256 devices in a mesh: seq: 16 (over x_lo, z), tp: 16 (over x_hi, y, core).
Axes of the slice: x: 4 (x_hi: 2, x_lo: 2; x = x_hi * 2 + x_lo), y: 4, z: 8, core: 2. Of those that a mesh axis runs over, the one named last changes fastest.
Arguments:
- tokens: bfloat16 [8192, 2048], P('seq', 'tp'), may hold values from -6 to 6
- w_first: bfloat16 [16, 512, 512], P('seq'), may hold values from -0.25 to 0.25
- second_factor_weight: bfloat16 [512, 16, 16], P('seq'), may hold values from -1.5 to 1.5
- w_up: bfloat16 [64, 2, 128, 128], P('tp'), may hold values from -0.375 to 0.375
- w_self: bfloat16 [6, 64, 128, 128], P(None, 'tp'), may hold values from -0.375 to 0.375
- w_cross: bfloat16 [6, 64, 128, 128], P(None, 'tp'), may hold values from -0.375 to 0.375
- w_down: bfloat16 [64, 2, 128, 128], P('tp'), may hold values from -0.1875 to 0.1875
- block_pairs: int32 [64, 2], P('tp'), may hold values from 0 to 15, all different within a row
- cotangent: bfloat16 [8192, 2048], P('seq', 'tp'), may hold values from -6 to 6
Outputs:
- layer_out: bfloat16 [8192, 2048], P('seq', 'tp')
- grad_tokens: bfloat16 [8192, 2048], P('seq', 'tp')
- grad_first: float32 [16, 512, 512], P('seq')
- gradient_second_factor: float32 [512, 16, 16], P('seq')
- grad_self: float32 [6, 64, 128, 128], P(None, 'tp', 'seq')
- grad_cross: float32 [6, 64, 128, 128], P(None, 'tp', 'seq')
The draws below stay inside these ranges and needn't reach their ends.
Inputs may be any that keep to these rules, and one draw needn't show every extreme that they name: `block_pairs`: each row names two different input blocks, and every one of the 16 input blocks is named by some row.
All inputs are finite; a program needn't handle non-finite values.
Results may differ from the reference program's by a relative error of at most 0.019.
Values may be sent and summed in bfloat16 or wider, within the bound.
No kernel may reach another device: no remote copies, remote signals or barrier semaphores. Data moves between devices by JAX's collectives and lax.ppermute only.
A program may use at most 64 MiB of HBM per device.

```python
import math
import jax
import jax.numpy as jnp
from jax import lax

MODEL_DIMENSION = 2048
BLK = 128
B = 512
LEVELS = 6
SEQ_DEV = 512
SEQUENCE_TOKENS = 8192
NB = 16
HB = 64
IB = 16
N_SEQ = 16


def levels(rng, shape, cuts, smallest, top_value):
    def one(dim, parts):
        steps = jax.random.uniform(jax.random.fold_in(jax.random.fold_in(rng, 6), dim), (parts,), jnp.float32, smallest / len(cuts), top_value / len(cuts))
        return jnp.repeat(jnp.exp(steps), shape[dim] // parts).reshape((-1,) + (1,) * (len(shape) - dim - 1))

    loudness = one(*cuts[0])
    for cut in cuts[1:]:
        loudness = loudness * one(*cut)
    return loudness


def picks_of(rng, rows, number_of, top, lift):
    order = jax.random.permutation(jax.random.fold_in(rng, 1), number_of)
    favour = order
    for power in range(3):
        favour = favour * favour // number_of
    favour = favour * lift // number_of
    tickets = jax.random.randint(jax.random.fold_in(rng, 2), (rows, number_of), 0, 4096) + favour
    holders = jax.random.permutation(jax.random.fold_in(rng, 3), rows)[jnp.arange(number_of) % rows]
    tickets = jnp.where(jnp.arange(rows)[:, None] == holders[None, :], 1 << 14, tickets)
    merit = tickets * number_of + jnp.arange(number_of)
    return lax.top_k(merit.astype(jnp.int32), top)[1].astype(jnp.int32)


def noise(key, extent, scale, limit, split=(), kind=jnp.bfloat16):
    entries = jax.random.normal(key, extent, jnp.float32) * scale
    if len(split) > 0:
        entries = levels(key, extent, split, -0.22, 0.18) * entries
    return jnp.clip(entries, min=-limit, max=limit).astype(kind)


def setup_inputs(seed: int = 0) -> dict:
    arg_keys = jax.random.split(jax.random.key(seed), 10)
    return {
        "tokens": noise(arg_keys[0], (SEQUENCE_TOKENS, MODEL_DIMENSION), 1.0, 6.0, ((0, 16), (1, 16))),
        "w_first": noise(arg_keys[1], (NB, B, B), B ** -0.5, 0.25, ((0, 16),)),
        "second_factor_weight": noise(arg_keys[2], (B, NB, NB), NB ** -0.5, 1.5, ((0, 16),)),
        "w_up": noise(arg_keys[3], (HB, 2, BLK, BLK), (2 * BLK) ** -0.5, 0.375, ((0, 16),)),
        "w_self": noise(arg_keys[4], (LEVELS, HB, BLK, BLK), (2 * BLK) ** -0.5, 0.375, ((1, 16),)),
        "w_cross": noise(arg_keys[5], (LEVELS, HB, BLK, BLK), (2 * BLK) ** -0.5, 0.375, ((1, 16),)),
        "w_down": noise(arg_keys[6], (HB, 2, BLK, BLK), (2 * HB * BLK // IB) ** -0.5, 0.1875, ((0, 16),)),
        "block_pairs": picks_of(arg_keys[7], HB, IB, 2, 0),
        "cotangent": noise(arg_keys[8], (SEQUENCE_TOKENS, MODEL_DIMENSION), 1.0, 6.0, ((0, 16), (1, 16))),
    }


def gelu_tanh(value):
    return jax.nn.gelu(value, approximate=True)

def swap_partner(state, level):
    span = 2 ** level
    shape = state.shape
    folded = state.reshape(shape[0], shape[1] // (2 * span), 2, span, shape[2])
    return jnp.flip(folded, axis=2).reshape(shape)

def reference(tokens, w_first, second_factor_weight, w_up, w_self, w_cross, w_down, block_pairs, cotangent):
    grouped = tokens.reshape(NB, B, MODEL_DIMENSION).astype(jnp.float32)
    first_factor_output = jnp.einsum('acb,abd->acd', w_first.astype(jnp.float32), grouped).astype(jnp.bfloat16)
    mixed_tokens = jnp.einsum('vyi,ivz->yvz', second_factor_weight.astype(jnp.float32), first_factor_output.astype(jnp.float32)).astype(jnp.bfloat16).reshape(SEQUENCE_TOKENS, MODEL_DIMENSION)
    hidden_in = (tokens.astype(jnp.float32) + mixed_tokens.astype(jnp.float32)).astype(jnp.bfloat16)
    flat_pairs = block_pairs.reshape(-1)
    chosen = (block_pairs[:, :, None] == jnp.arange(IB, dtype=jnp.int32)[None, None, :]).astype(jnp.float32)
    up_full = w_up.astype(jnp.float32)
    down_full = w_down.astype(jnp.float32)
    self_full = w_self.astype(jnp.float32)
    cross_full = w_cross.astype(jnp.float32)

    def mlp_block(carry, rows_in):
        grads_self, grads_cross = carry
        hid_rows, cot_rows = rows_in
        count = hid_rows.shape[0]
        picked = jnp.take(hid_rows.reshape(count, IB, BLK), flat_pairs, axis=1).reshape(count, HB, 2, BLK)
        state = jnp.einsum('rjkc,jkce->rje', picked.astype(jnp.float32), up_full).astype(jnp.bfloat16)
        states = [state]
        for level_at in range(LEVELS):
            partner = swap_partner(state, level_at)
            state = (jnp.einsum('rjc,jce->rje', state.astype(jnp.float32), self_full[level_at]) + jnp.einsum('rjc,jce->rje', partner.astype(jnp.float32), cross_full[level_at])).astype(jnp.bfloat16)
            states.append(state)
        top = state.astype(jnp.float32)
        activated = gelu_tanh(top).astype(jnp.bfloat16)
        pieces = jnp.einsum('rjc,jkce->rjke', activated.astype(jnp.float32), down_full)
        down_out = jnp.einsum('rjke,jki->rie', pieces, chosen).reshape(count, MODEL_DIMENSION)
        layer_rows = (hid_rows.astype(jnp.float32) + down_out).astype(jnp.bfloat16)
        grad_picked = jnp.take(cot_rows.reshape(count, IB, BLK), flat_pairs, axis=1).reshape(count, HB, 2, BLK)
        grad_act = jnp.einsum('rjke,jkce->rjc', grad_picked.astype(jnp.float32), down_full)
        _, pull = jax.vjp(gelu_tanh, top)
        grad_state = pull(grad_act)[0].astype(jnp.bfloat16)
        self_terms = [None] * LEVELS
        cross_terms = [None] * LEVELS
        for level_at in reversed(range(LEVELS)):
            below = states[level_at].astype(jnp.float32)
            upper = grad_state.astype(jnp.float32)
            self_terms[level_at] = jnp.einsum('rjc,rje->jce', below, upper)
            cross_terms[level_at] = jnp.einsum('rjc,rje->jce', swap_partner(below, level_at), upper)
            across = jnp.einsum('rje,jce->rjc', upper, cross_full[level_at])
            grad_state = (jnp.einsum('rje,jce->rjc', upper, self_full[level_at]) + swap_partner(across, level_at)).astype(jnp.bfloat16)
        back_pieces = jnp.einsum('rje,jkce->rjkc', grad_state.astype(jnp.float32), up_full)
        spread = jnp.einsum('rjkc,jki->ric', back_pieces, chosen).reshape(count, MODEL_DIMENSION)
        grad_rows = (cot_rows.astype(jnp.float32) + spread).astype(jnp.bfloat16)
        carry_out = (grads_self + jnp.stack(self_terms), grads_cross + jnp.stack(cross_terms))
        return (carry_out, (layer_rows, grad_rows))
    zeros_start = jnp.zeros((LEVELS, HB, BLK, BLK), jnp.float32)
    sums, outputs = lax.scan(mlp_block, (zeros_start, zeros_start), (hidden_in.reshape(N_SEQ, SEQ_DEV, MODEL_DIMENSION), cotangent.reshape(N_SEQ, SEQ_DEV, MODEL_DIMENSION)))
    layer_out = outputs[0].reshape(SEQUENCE_TOKENS, MODEL_DIMENSION)
    grad_hidden = outputs[1].reshape(SEQUENCE_TOKENS, MODEL_DIMENSION)
    token_scale = 1.0 / math.sqrt(SEQUENCE_TOKENS)
    model_width_scale = 1.0 / math.sqrt(MODEL_DIMENSION)
    gradient_group_rows = grad_hidden.reshape(NB, B, MODEL_DIMENSION).astype(jnp.float32)
    gradient_first_output = jnp.einsum('emj,meg->jeg', second_factor_weight.astype(jnp.float32), gradient_group_rows).astype(jnp.bfloat16)
    gradient_second_factor = jnp.einsum('tfm,lfm->ftl', gradient_group_rows, first_factor_output.astype(jnp.float32)) * model_width_scale
    grad_first = jnp.einsum('acd,abd->acb', gradient_first_output.astype(jnp.float32), grouped) * model_width_scale
    grad_mix = jnp.einsum('acb,acd->abd', w_first.astype(jnp.float32), gradient_first_output.astype(jnp.float32)).reshape(SEQUENCE_TOKENS, MODEL_DIMENSION)
    grad_tokens = (grad_hidden.astype(jnp.float32) + grad_mix).astype(jnp.bfloat16)
    return (layer_out, grad_tokens, grad_first, gradient_second_factor, sums[0] * token_scale, sums[1] * token_scale)
```

```python
import functools
import math

import jax
import jax.numpy as jnp
from jax import lax
from jax.experimental import pallas as pl
from jax.experimental.pallas import tpu as pltpu
from jax.sharding import PartitionSpec as P


BF = jnp.bfloat16
F32 = jnp.float32
CHUNKS = 2
MIB = 1 << 20


def _send(value, axis, target):
    return lax.ppermute(value, axis, [(s, target(s)) for s in range(16)])


def _xor(mask):
    return lambda t: t ^ mask


def _ymove(step):
    return lambda t: (t & 9) | (((((t >> 1) & 3) + step) & 3) << 1)


CORE, XHI = _xor(1), _xor(8)


def gather_tp(block):
    own = block[None]
    across = _send(own, "tp", XHI)
    far = _send(own, "tp", _ymove(2))
    pair = jnp.concatenate([own, across], 0)
    below = _send(pair, "tp", _ymove(1))
    above = _send(pair, "tp", _ymove(3))
    far_across = _send(far, "tp", XHI)
    mine = (pair, far, below, above, far_across)
    return mine + tuple(_send(v, "tp", CORE) for v in mine)


GATHER_SIZES = (2, 1, 2, 2, 1) * 2


def position(block):
    me = lax.axis_index("tp")
    dx = ((block ^ me) >> 3) & 1
    dc = (block ^ me) & 1
    dy = ((block >> 1) - (me >> 1)) & 3
    key = dx * 4 + dy
    order = jnp.zeros_like(key)
    for k, at in enumerate((0, 5, 2, 3, 1, 6, 7, 4)):
        order = order + jnp.where(key == k, at, 0)
    return (order + 8 * dc).astype(jnp.int32)


def _call(body, outs, args, specs=None, scratch=(), flops=0, limit=24):
    specs = specs or [None] * len(args)
    full = lambda a: pl.BlockSpec(a.shape, lambda i, n=len(a.shape): (0,) * n)
    in_specs = [s if s is not None else full(a) for s, a in zip(specs, args)]
    moved = sum(a.size * a.dtype.itemsize for a in args) + sum(
        o.size * o.dtype.itemsize for o in outs
    )
    out = pl.pallas_call(
        body,
        grid=(1,),
        in_specs=in_specs,
        out_specs=[full(o) for o in outs],
        out_shape=list(outs),
        scratch_shapes=list(scratch),
        compiler_params=pltpu.CompilerParams(vmem_limit_bytes=limit * MIB),
        cost_estimate=pl.CostEstimate(
            flops=flops, bytes_accessed=moved, transcendentals=0
        ),
    )(*args)
    return out


def _shape(*shape, dtype=BF):
    return jax.ShapeDtypeStruct(shape, dtype)


SMEM = pl.BlockSpec(memory_space=pltpu.SMEM)


def _dot(a, b):
    return lax.dot_general(a, b, (((1,), (0,)), ((), ())), preferred_element_type=F32)


def _dot_t(a, b):
    return lax.dot_general(a, b, (((1,), (1,)), ((), ())), preferred_element_type=F32)


def _dot_l(a, b):
    return lax.dot_general(a, b, (((0,), (0,)), ((), ())), preferred_element_type=F32)


def _cat(a, b):
    return jnp.concatenate([a, b], axis=1)


def chunk_specs(blocks, chunk, tokens, plane=None):
    if plane is None:
        return [
            pl.BlockSpec((b.shape[0], tokens, 128), lambda i: (0, chunk, 0))
            for b in blocks
        ]
    return [
        pl.BlockSpec((b.shape[0], None, tokens, 128), lambda i: (0, plane, chunk, 0))
        for b in blocks
    ]


def up_levels(where, blocks, chunk, tokens, w_up, w_near):
    slots = w_up.shape[0]

    def body(where_ref, *refs):
        ins, (up, near, s0, s1, s2, held) = refs[: len(blocks)], refs[len(blocks) :]
        at = 0
        for ref in ins:
            for i in range(ref.shape[0]):
                held[at] = ref[i]
                at += 1
        for j in range(slots):
            left, right = held[where_ref[2 * j]], held[where_ref[2 * j + 1]]
            s0[j] = _dot(_cat(left, right), up[j]).astype(BF)
        for level, (src, dst) in enumerate(((s0, s1), (s1, s2))):
            for j in range(slots):
                both = _cat(src[j], src[j ^ (1 << level)])
                dst[j] = _dot(both, near[level, j]).astype(BF)

    return _call(
        body,
        [_shape(slots, tokens, 128)] * 3,
        (where, *blocks, w_up, w_near),
        [SMEM, *chunk_specs(blocks, chunk, tokens), None, None],
        scratch=[pltpu.VMEM((16, tokens, 128), BF)],
        flops=3 * slots * tokens * 2 * 256 * 128,
    )


def level_up(state, partner, weight):
    slots, tokens, _ = state.shape

    def body(s, p, w, out):
        for j in range(slots):
            out[j] = _dot(_cat(s[j], p[j]), w[j]).astype(BF)

    return _call(
        body,
        [_shape(*state.shape)],
        (state, partner, weight),
        flops=slots * tokens * 2 * 256 * 128,
    )[0]


def gather_grad(where, blocks, chunk, tokens, w_down):
    slots = w_down.shape[0]

    def body(where_ref, *refs):
        ins, (down, out, held) = refs[: len(blocks)], refs[len(blocks) :]
        at = 0
        for ref in ins:
            for i in range(ref.shape[0]):
                held[at] = ref[i]
                at += 1
        for j in range(slots):
            total = _dot_t(held[where_ref[2 * j]], down[j, 0])
            out[j] = total + _dot_t(held[where_ref[2 * j + 1]], down[j, 1])

    return _call(
        body,
        [_shape(slots, tokens, 128, dtype=F32)],
        (where, *blocks, w_down),
        [SMEM, *chunk_specs(blocks, chunk, tokens, 1), None],
        scratch=[pltpu.VMEM((16, tokens, 128), BF)],
        flops=slots * tokens * 4 * 128 * 128,
    )[0]


ROOT = math.sqrt(2.0 / math.pi)


def top_level(state, partner, weight, grad_act, cross):
    slots, tokens, _ = state.shape

    def body(s, p, w, ga, wc, act, grad, across):
        for j in range(slots):
            v = _dot(_cat(s[j], p[j]), w[j]).astype(BF).astype(F32)
            square = v * v
            t = jnp.tanh(ROOT * (v + 0.044715 * (v * square)))
            act[j] = (0.5 * v * (1.0 + t)).astype(BF)
            slope = 0.5 * (1.0 + t) + (0.5 * ROOT) * v * (1.0 - t * t) * (
                1.0 + (3 * 0.044715) * square
            )
            g = (ga[j] * slope).astype(BF)
            grad[j] = g
            across[j] = _dot_t(g, wc[j]).astype(BF)

    return _call(
        body,
        [_shape(*state.shape)] * 3,
        (state, partner, weight, grad_act, cross),
        flops=slots * tokens * 3 * 2 * 128 * 128,
    )


def level_down(grad, incoming, w_self, cross):
    slots, tokens, _ = grad.shape

    def body(g, inc, w, wc, out, across):
        for j in range(slots):
            new = (_dot_t(g[j], w[j]) + inc[j].astype(F32)).astype(BF)
            out[j] = new
            across[j] = _dot_t(new, wc[j]).astype(BF)

    return _call(
        body,
        [_shape(*grad.shape)] * 2,
        (grad, incoming, w_self, cross),
        flops=slots * tokens * 2 * 2 * 128 * 128,
    )


def _scatter(where_ref, pieces, total, keep, send):
    total[...] = jnp.zeros_like(total)
    for i, piece in pieces:
        at = where_ref[i]
        total[at] = total[at] + piece()
    keep[...] = total[0:8].astype(BF)
    send[...] = total[8:16].astype(BF)


def bottom_levels(where, grad, incoming, w_self, near_self, near_cross, w_up):
    slots, tokens, _ = grad.shape

    def body(where_ref, g, inc, w, ws, wc, up, g2, g1, keep, send, g0, total):
        for j in range(slots):
            g2[j] = (_dot_t(g[j], w[j]) + inc[j].astype(F32)).astype(BF)
        for level, (src, dst) in ((1, (g2, g1)), (0, (g1, g0))):
            for j in range(slots):
                other = j ^ (1 << level)
                new = _dot_t(src[j], ws[level, j])
                dst[j] = (new + _dot_t(src[other], wc[level, other])).astype(BF)
        pieces = [
            (2 * j + k, functools.partial(lambda j, k: _dot_t(g0[j], up[j, k]), j, k))
            for j in range(slots)
            for k in range(2)
        ]
        _scatter(where_ref, pieces, total, keep, send)

    return _call(
        body,
        [_shape(slots, tokens, 128)] * 2 + [_shape(8, tokens, 128)] * 2,
        (where, grad, incoming, w_self, near_self, near_cross, w_up),
        [SMEM] + [None] * 6,
        scratch=[
            pltpu.VMEM((slots, tokens, 128), BF),
            pltpu.VMEM((16, tokens, 128), F32),
        ],
        flops=slots * tokens * 7 * 2 * 128 * 128,
    )


def down_pieces(where, activated, w_down):
    slots, tokens, _ = activated.shape

    def body(where_ref, act, down, keep, send, total):
        pieces = [
            (2 * j + k, functools.partial(lambda j, k: _dot(act[j], down[j, k]), j, k))
            for j in range(slots)
            for k in range(2)
        ]
        _scatter(where_ref, pieces, total, keep, send)

    return _call(
        body,
        [_shape(8, tokens, 128)] * 2,
        (where, activated, w_down),
        [SMEM, None, None],
        scratch=[pltpu.VMEM((16, tokens, 128), F32)],
        flops=slots * tokens * 2 * 2 * 128 * 128,
    )


def scatter_tp(keeps, sends):
    got = [_send(v, "tp", CORE) for v in sends]
    tokens = sum(v.shape[1] for v in keeps)
    n = len(keeps)

    def first(*refs):
        kept, came, (own, two, up, down, side) = refs[:n], refs[n : 2 * n], refs[2 * n :]
        start = 0
        for k, g in zip(kept, came):
            rows = pl.ds(start, k.shape[1])
            start += k.shape[1]
            part = lambda i: k[i].astype(F32) + g[i].astype(F32)
            own[rows] = part(0)
            two[0, rows] = part(1)
            two[1, rows] = part(2)
            for i in range(2):
                down[i, rows] = part(3 + i).astype(BF)
                up[i, rows] = part(5 + i).astype(BF)
            side[0, rows] = part(7).astype(BF)

    own, two, up, down, side = _call(
        first,
        [
            _shape(tokens, 128, dtype=F32),
            _shape(2, tokens, 128, dtype=F32),
            _shape(2, tokens, 128),
            _shape(2, tokens, 128),
            _shape(1, tokens, 128),
        ],
        (*keeps, *got),
        flops=1,
    )
    from_below = _send(up, "tp", _ymove(1))
    from_above = _send(down, "tp", _ymove(3))
    from_side = _send(side, "tp", XHI)

    def second(two, below, above, side, to_side, to_far):
        to_side[...] = (
            two[0] + below[1].astype(F32) + above[1].astype(F32)
        ).astype(BF)
        to_far[...] = (two[1] + side[0].astype(F32)).astype(BF)

    to_side, to_far = _call(
        second,
        [_shape(tokens, 128)] * 2,
        (two, from_below, from_above, from_side),
        flops=1,
    )
    last_side = _send(to_side, "tp", XHI)
    last_far = _send(to_far, "tp", _ymove(2))
    return own, from_below, from_above, last_side, last_far


def add_up(base, terms, others=()):
    tokens = base.shape[0]

    def body(base, own, below, above, side, far, out):
        total = own[...] + below[0].astype(F32) + above[0].astype(F32)
        total = total + side[...].astype(F32) + far[...].astype(F32)
        out[...] = (base[...].astype(F32) + total).astype(BF)

    return _call(body, [_shape(tokens, 128)], (base, *terms), flops=1)[0]


def outer_terms(me, lefts, rights, grads):
    flat, plan = [], []
    for left, right, grad in zip(lefts, rights, grads):
        entry = []
        for c in range(len(left)):
            first = len(flat)
            flat.append(left[c])
            if not isinstance(right, int):
                flat.append(right[c])
            flat.append(grad[c])
            entry.append(first)
        plan.append((entry, right if isinstance(right, int) else 0))
    slots = lefts[0][0].shape[0]
    mats = len(plan) * 2 * slots
    n = len(flat)

    def body(me_ref, *refs):
        ins, (keep, send, held) = refs[:n], refs[n:]
        for level, (entry, span) in enumerate(plan):
            for j in range(slots):
                total = None
                for first in entry:
                    left = ins[first][j]
                    if span:
                        right, grad = ins[first][j ^ span], ins[first + 1][j]
                    else:
                        right, grad = ins[first + 1][j], ins[first + 2][j]
                    term = _dot_l(_cat(left, right), grad)
                    total = term if total is None else total + term
                held[...] = total
                for half in range(2):
                    mat = (level * 2 + half) * slots + j
                    for pos in range(16):
                        z0, xl, z1, z2 = pos >> 3, (pos >> 2) & 1, (pos >> 1) & 1, pos & 1
                        rel = xl * 8 + z2 * 4 + z1 * 2 + z0
                        row = half * 128 + (me_ref[0] ^ rel) * 8
                        value = held[pl.ds(pl.multiple_of(row, 8), 8), :]
                        if pos < 8:
                            keep[pos, mat] = value
                        else:
                            send[pos - 8, mat] = value.astype(BF)

    return _call(
        body,
        [_shape(8, mats, 8, 128, dtype=F32), _shape(8, mats, 8, 128)],
        (me, *flat),
        [SMEM] + [None] * n,
        scratch=[pltpu.VMEM((256, 128), F32)],
        flops=len(plan) * slots * len(plan[0][0]) * flat[0].shape[1] * 2 * 256 * 128,
    )


def halve_seq(keep, send, scale):
    for mask in (1, 8, 2, 4):
        came = _send(send, "seq", _xor(mask))
        size = keep.shape[0] // 2

        def body(k, c, new_keep, new_send):
            new_keep[...] = k[:size] + c[:size].astype(F32)
            new_send[...] = (k[size:] + c[size:].astype(F32)).astype(BF)

        def final(k, c, out):
            out[...] = (k[...] + c[...].astype(F32)) * scale

        if size:
            tail = keep.shape[1:]
            keep, send = _call(
                body,
                [_shape(size, *tail, dtype=F32), _shape(size, *tail)],
                (keep, came),
                flops=1,
            )
        else:
            keep = _call(final, [_shape(*keep.shape, dtype=F32)], (keep, came), flops=1)[0]
    return keep[0]


def _mask(shape):
    row = lax.broadcasted_iota(jnp.int32, shape, 0)
    col = lax.broadcasted_iota(jnp.int32, shape, 1)
    return ((row ^ col) & 31) == 0


def _spread(shape):
    row = lax.broadcasted_iota(jnp.int32, shape, 0)
    col = lax.broadcasted_iota(jnp.int32, shape, 1)
    return (col >> 5) == row


def _expand(factor):
    n, groups = factor.shape
    wide = _dot(factor, _spread((groups, n)).astype(BF))
    return jnp.where(_mask((n, n)), wide, 0.0).astype(BF)


def mix(factor, rows):
    def body(f, r, out):
        out[...] = _dot(_expand(f[...]), r[...]).astype(BF)

    return _call(
        body, [_shape(*rows.shape)], (factor, rows), flops=2 * 512 * 512 * 128
    )[0]


def second_terms(grads, rows):
    def body(g, r, out):
        n = r.shape[0]
        both = _dot_t(r[...], g[...])
        both = jnp.where(_mask((n, n)), both, 0.0)
        pick = _spread((16, n)).astype(F32)
        small = lax.dot_general(
            pick,
            both,
            (((1,), (0,)), ((), ())),
            precision=lax.Precision.HIGHEST,
            preferred_element_type=F32,
        )
        for k in range(4):
            out[k * 16 : k * 16 + 16, :] = small[:, k * 128 : k * 128 + 128].astype(BF)

    return _call(body, [_shape(64, 128)], (grads, rows), flops=2 * 512 * 512 * 128)[0]


def first_grad(grads, tokens, scale):
    n = len(grads)

    def body(*refs):
        gs, ts, (out, small) = refs[:n], refs[n : 2 * n], refs[2 * n :]
        total, extra = None, None
        g_list = [(r, i) for r in gs for i in range(r.shape[0])]
        t_list = [(r, i) for r in ts for i in range(r.shape[0])]
        for at in range(0, len(g_list), 2):
            (ga, ia), (gb, ib) = g_list[at], g_list[at + 1]
            (ta, ja), (tb, jb) = t_list[at], t_list[at + 1]
            left = _cat(ga[ia, 0:512, :], gb[ib, 0:512, :])
            term = _dot_t(left, _cat(ta[ja], tb[jb]))
            total = term if total is None else total + term
            for r, i in ((ga, ia), (gb, ib)):
                part = r[i, 512:576, :].astype(F32)
                extra = part if extra is None else extra + part
        out[...] = total * scale
        small[...] = extra * scale

    specs = [
        pl.BlockSpec(g.shape, lambda i: (0, 0, 0)) for g in grads
    ] + chunk_specs(tokens, 0, 512, 0)
    return _call(
        body,
        [_shape(512, 512, dtype=F32), _shape(64, 128, dtype=F32)],
        (*grads, *tokens),
        specs,
        flops=2 * 512 * 512 * 2048,
        limit=40,
    )


def per_device(
    tokens, w_first, second_factor, w_up, w_self, w_cross, w_down, block_pairs, cotangent
):
    seq_len, width = tokens.shape
    levels, slots = w_self.shape[:2]
    token_scale = 1.0 / math.sqrt(seq_len * lax.axis_size("seq"))
    width_scale = 1.0 / math.sqrt(width * lax.axis_size("tp"))
    size = seq_len // CHUNKS
    chunks = range(CHUNKS)
    me = lax.axis_index("seq").astype(jnp.int32).reshape(1)
    where = position(block_pairs.reshape(-1))
    stacked = jnp.concatenate([w_self, w_cross], axis=2)
    up_stacked = w_up.reshape(slots, 256, 128)
    factor = second_factor.transpose(1, 0, 2).reshape(512, 16)
    factor_t = second_factor.transpose(2, 0, 1).reshape(512, 16)

    def swap_seq(rows):
        moved = lax.all_to_all(
            rows.reshape(16, 32, 128), "seq", split_axis=0, concat_axis=0, tiled=True
        )
        return moved.reshape(512, 128)

    first_out = jnp.dot(w_first[0], tokens, preferred_element_type=F32).astype(BF)
    first_rows = swap_seq(first_out)
    early = gather_tp(jnp.stack([tokens, cotangent]))
    mixed = swap_seq(mix(factor, first_rows))
    hidden = (tokens.astype(F32) + mixed.astype(F32)).astype(BF)
    blocks = gather_tp(hidden)

    partner_of = [None, None] + [_xor(1 << b) for b in range(levels - 2)]
    states = [[None] * CHUNKS for _ in range(levels)]
    partners = [[None] * CHUNKS for _ in range(levels)]
    grads = [[None] * CHUNKS for _ in range(levels + 1)]
    keeps, sends, acts = [None] * CHUNKS, [None] * CHUNKS, [None] * CHUNKS
    grad_act = [gather_grad(where, early, c, size, w_down) for c in chunks]
    for c in chunks:
        s0, s1, s2 = up_levels(where, blocks, c, size, up_stacked, stacked[:2])
        states[0][c], states[1][c], states[2][c] = s0, s1, s2
    for level in range(2, levels):
        for c in chunks:
            state = states[level][c]
            partner = _send(state, "tp", partner_of[level])
            partners[level][c] = partner
            if level + 1 < levels:
                states[level + 1][c] = level_up(state, partner, stacked[level])
    incoming = [None] * CHUNKS
    for c in chunks:
        top = levels - 1
        acts[c], grads[levels][c], across = top_level(
            states[top][c], partners[top][c], stacked[top], grad_act[c], w_cross[top]
        )
        incoming[c] = _send(across, "tp", partner_of[top])
    for level in range(levels - 1, 2, -1):
        for c in chunks:
            grads[level][c], across = level_down(
                grads[level + 1][c], incoming[c], w_self[level], w_cross[level - 1]
            )
            incoming[c] = _send(across, "tp", partner_of[level - 1])
    for c in chunks:
        grads[2][c], grads[1][c], keeps[c], sends[c] = bottom_levels(
            where, grads[3][c], incoming[c], w_self[2], w_self[:2], w_cross[:2], w_up
        )
    grad_hidden = add_up(cotangent, scatter_tp(keeps, sends))

    upper = outer_terms(me, states[3:6], partners[3:6], grads[4:7])
    upper = halve_seq(*upper, token_scale)
    lower = outer_terms(me, states[0:3], [1, 2, partners[2]], grads[1:4])
    lower = halve_seq(*lower, token_scale)

    grad_rows = swap_seq(grad_hidden)
    grad_first_out = swap_seq(mix(factor_t, grad_rows))
    extra = second_terms(grad_rows, first_rows)
    late = gather_tp(jnp.concatenate([grad_first_out, extra], 0))
    grad_mix = lax.dot_general(
        w_first[0], grad_first_out, (((0,), (0,)), ((), ())), preferred_element_type=F32
    )
    grad_tokens = (grad_hidden.astype(F32) + grad_mix).astype(BF)

    acts, _ = lax.optimization_barrier((acts, grad_hidden))
    pieces = [down_pieces(where, acts[c], w_down) for c in chunks]
    layer_out = add_up(hidden, scatter_tp([p[0] for p in pieces], [p[1] for p in pieces]))

    grad_first, small = first_grad(late, early, width_scale)
    grad_second = (
        small.reshape(4, 16, 4, 32).transpose(3, 0, 2, 1).reshape(32, 16, 16)
    )
    both = jnp.concatenate(
        [lower.reshape(3, 2, slots, 8, 128), upper.reshape(3, 2, slots, 8, 128)], 0
    )
    return (
        layer_out,
        grad_tokens,
        grad_first[None],
        grad_second,
        both[:, 0],
        both[:, 1],
    )


def solution(mesh):
    in_specs = (
        P("seq", "tp"),
        P("seq", None, None),
        P("seq", None, None),
        P("tp", None, None, None),
        P(None, "tp", None, None),
        P(None, "tp", None, None),
        P("tp", None, None, None),
        P("tp", None),
        P("seq", "tp"),
    )
    out_specs = (
        P("seq", "tp"),
        P("seq", "tp"),
        P("seq", None, None),
        P("seq", None, None),
        P(None, "tp", "seq", None),
        P(None, "tp", "seq", None),
    )
    return jax.shard_map(
        per_device, mesh=mesh, in_specs=in_specs, out_specs=out_specs, check_vma=False
    )
```

```python
import math

import jax
import jax.numpy as jnp
from jax import lax
from jax.experimental import pallas as pl
from jax.experimental.pallas import tpu as pltpu
from jax.sharding import PartitionSpec as P


BF = jnp.bfloat16
F32 = jnp.float32
MIB = 1 << 20
ROOT = math.sqrt(2.0 / math.pi)


def _send(value, axis, target):
    return lax.ppermute(value, axis, [(s, target(s)) for s in range(16)])


def _xor(mask):
    return lambda t: t ^ mask


def _ymove(step):
    return lambda t: (t & 9) | (((((t >> 1) & 3) + step) & 3) << 1)


CORE, XHI = _xor(1), _xor(8)


def after(value, *others):
    return lax.optimization_barrier((value, others))[0]


def position(block):
    me = lax.axis_index("tp")
    dx = ((block ^ me) >> 3) & 1
    dc = (block ^ me) & 1
    dy = ((block >> 1) - (me >> 1)) & 3
    key = dx * 4 + dy
    order = jnp.zeros_like(key)
    for k, at in enumerate((0, 4, 6, 2, 1, 5, 7, 3)):
        order = order + jnp.where(key == k, at, 0)
    return (order + 8 * dc).astype(jnp.int32)


def _shape(*shape, dtype=BF):
    return jax.ShapeDtypeStruct(shape, dtype)


VMEM = pl.BlockSpec(memory_space=pltpu.VMEM)
SMEM = pl.BlockSpec(memory_space=pltpu.SMEM)


def _call(body, outs, args, scalars=0, scratch=(), flops=0, limit=8):
    moved = sum(a.size * a.dtype.itemsize for a in args) + sum(
        math.prod(o.shape) * o.dtype.itemsize for o in outs
    )
    return pl.pallas_call(
        body,
        in_specs=[SMEM] * scalars + [VMEM] * (len(args) - scalars),
        out_specs=[VMEM] * len(outs),
        out_shape=list(outs),
        scratch_shapes=list(scratch),
        compiler_params=pltpu.CompilerParams(vmem_limit_bytes=limit * MIB),
        cost_estimate=pl.CostEstimate(
            flops=flops, bytes_accessed=moved, transcendentals=0
        ),
    )(*args)


def _dot(a, b):
    return lax.dot_general(a, b, (((1,), (0,)), ((), ())), preferred_element_type=F32)


def _dot_t(a, b):
    return lax.dot_general(a, b, (((1,), (1,)), ((), ())), preferred_element_type=F32)


def _dot_l(a, b):
    return lax.dot_general(a, b, (((0,), (0,)), ((), ())), preferred_element_type=F32)


def _cat(a, b):
    return jnp.concatenate([a, b], axis=1)


def _stack(a, b):
    return jnp.concatenate([a, b], axis=0)


def join(*pieces):
    total = sum(p.shape[0] for p in pieces)

    def body(*refs):
        at = 0
        for ref in refs[:-1]:
            refs[-1][at : at + ref.shape[0]] = ref[...]
            at += ref.shape[0]

    return _call(body, [_shape(total, *pieces[0].shape[1:])], pieces)[0]


def gather_y(pair):
    return (
        _send(pair, "tp", _ymove(1)),
        _send(pair, "tp", _ymove(3)),
        _send(pair, "tp", _ymove(2)),
    )


def gather_core(*pieces):
    own = join(*pieces)
    return own, _send(own, "tp", CORE)


def _hold(refs, held, start, rows):
    at = 0
    for ref in refs:
        for i in range(ref.shape[0]):
            held[at] = ref[i, start : start + rows, :]
            at += 1


def up_levels(where, blocks, w_up, w_self, w_cross):
    slots, tokens = w_up.shape[0], blocks[0].shape[1]
    n = len(blocks)

    def body(where_ref, *refs):
        ins, (up, ws, wc, s0, s1, s2, held) = refs[:n], refs[n:]
        _hold(ins, held, 0, tokens)
        for j in range(slots):
            left, right = held[where_ref[2 * j]], held[where_ref[2 * j + 1]]
            s0[j] = _dot(_cat(left, right), _stack(up[j, 0], up[j, 1])).astype(BF)
        for level, (src, dst) in enumerate(((s0, s1), (s1, s2))):
            for j in range(slots):
                both = _cat(src[j], src[j ^ (1 << level)])
                dst[j] = _dot(both, _stack(ws[level, j], wc[level, j])).astype(BF)

    return _call(
        body,
        [_shape(slots, tokens, 128)] * 3,
        (where, *blocks, w_up, w_self, w_cross),
        scalars=1,
        scratch=[pltpu.VMEM((16, tokens, 128), BF)],
        flops=3 * slots * tokens * 2 * 256 * 128,
    )


def level_up(state, partner, w_self, w_cross, level, parts=1):
    slots, tokens, _ = state.shape
    rows = tokens // parts

    def body(s, p, ws, wc, *outs):
        for c, out in enumerate(outs):
            at = slice(c * rows, c * rows + rows)
            for j in range(slots):
                both = _cat(s[j, at, :], p[j, at, :])
                out[j] = _dot(both, _stack(ws[level, j], wc[level, j])).astype(BF)

    return _call(
        body,
        [_shape(slots, rows, 128)] * parts,
        (state, partner, w_self, w_cross),
        flops=slots * tokens * 2 * 256 * 128,
    )


def gather_grad(where, blocks, w_down, start, parts):
    slots = w_down.shape[0]
    tokens = blocks[0].shape[1] - start
    rows = tokens // parts
    n = len(blocks)

    def body(where_ref, *refs):
        ins, down, outs, held = refs[:n], refs[n], refs[n + 1 : -1], refs[-1]
        _hold(ins, held, start, tokens)
        for j in range(slots):
            left, right = held[where_ref[2 * j]], held[where_ref[2 * j + 1]]
            total = _dot_t(_cat(left, right), _cat(down[j, 0], down[j, 1]))
            for c, out in enumerate(outs):
                out[j] = total[c * rows : c * rows + rows]

    return _call(
        body,
        [_shape(slots, rows, 128, dtype=F32)] * parts,
        (where, *blocks, w_down),
        scalars=1,
        scratch=[pltpu.VMEM((16, tokens, 128), BF)],
        flops=slots * tokens * 4 * 128 * 128,
    )


def top_level(state, partner, w_self, w_cross, grad_act, level):
    slots, tokens, _ = state.shape

    def body(s, p, ws, wc, ga, act, grad, across):
        for j in range(slots):
            weight = _stack(ws[level, j], wc[level, j])
            v = _dot(_cat(s[j], p[j]), weight).astype(BF).astype(F32)
            square = v * v
            t = jnp.tanh(ROOT * (v + 0.044715 * (v * square)))
            act[j] = (0.5 * v * (1.0 + t)).astype(BF)
            slope = 0.5 * (1.0 + t) + (0.5 * ROOT) * v * (1.0 - t * t) * (
                1.0 + (3 * 0.044715) * square
            )
            g = (ga[j] * slope).astype(BF)
            grad[j] = g
            across[j] = _dot_t(g, wc[level, j]).astype(BF)

    return _call(
        body,
        [_shape(*state.shape)] * 3,
        (state, partner, w_self, w_cross, grad_act),
        flops=slots * tokens * 3 * 2 * 128 * 128,
    )


def level_down(grad, incoming, w_self, w_cross, level):
    slots, tokens, _ = grad.shape

    def body(g, inc, ws, wc, out, across):
        for j in range(slots):
            new = (_dot_t(g[j], ws[level, j]) + inc[j].astype(F32)).astype(BF)
            out[j] = new
            across[j] = _dot_t(new, wc[level - 1, j]).astype(BF)

    return _call(
        body,
        [_shape(*grad.shape)] * 2,
        (grad, incoming, w_self, w_cross),
        flops=slots * tokens * 2 * 2 * 128 * 128,
    )


def bottom_levels(where, grads, incoming, w_self, w_cross, w_up):
    parts = len(grads)
    slots, rows, _ = grads[0].shape
    tokens = rows * parts

    def body(where_ref, *refs):
        gs, incs = refs[:parts], refs[parts : 2 * parts]
        ws, wc, up, g2, g1, keep, send, g0, total = refs[2 * parts :]
        for c in range(parts):
            for j in range(slots):
                new = _dot_t(gs[c][j], ws[2, j]) + incs[c][j].astype(F32)
                g2[j, c * rows : c * rows + rows, :] = new.astype(BF)
        for level, (src, dst) in ((1, (g2, g1)), (0, (g1, g0))):
            for j in range(slots):
                other = j ^ (1 << level)
                both = _cat(src[j], src[other])
                weight = _cat(ws[level, j], wc[level, other])
                dst[j] = _dot_t(both, weight).astype(BF)
        total[...] = jnp.zeros_like(total)
        for j in range(slots):
            for k in range(2):
                at = where_ref[2 * j + k]
                total[at] = total[at] + _dot_t(g0[j], up[j, k])
        keep[...] = total[0:8].astype(BF)
        send[...] = total[8:16].astype(BF)

    return _call(
        body,
        [_shape(slots, tokens, 128)] * 2 + [_shape(8, tokens, 128)] * 2,
        (where, *grads, *incoming, w_self, w_cross, w_up),
        scalars=1,
        scratch=[
            pltpu.VMEM((slots, tokens, 128), BF),
            pltpu.VMEM((16, tokens, 128), F32),
        ],
        flops=slots * tokens * 7 * 2 * 128 * 128,
        limit=12,
    )


def down_pieces(where, acts, w_down):
    parts = len(acts)
    slots, rows, _ = acts[0].shape
    tokens = rows * parts

    def body(where_ref, *refs):
        ins, (down, keep, send, total) = refs[:parts], refs[parts:]
        total[...] = jnp.zeros_like(total)

        def step(j, carry):
            for c in range(parts):
                at = slice(c * rows, c * rows + rows)
                for k in range(2):
                    block = where_ref[2 * j + k]
                    total[block, at, :] = total[block, at, :] + _dot(
                        ins[c][j], down[j, k]
                    )
            return carry

        lax.fori_loop(0, slots, step, 0)
        keep[...] = total[0:8].astype(BF)
        send[...] = total[8:16].astype(BF)

    return _call(
        body,
        [_shape(8, tokens, 128)] * 2,
        (where, *acts, w_down),
        scalars=1,
        scratch=[pltpu.VMEM((16, tokens, 128), F32)],
        flops=slots * tokens * 2 * 2 * 128 * 128,
        limit=12,
    )


def scatter_one(keep, came):
    tokens = keep.shape[1]

    def body(k, g, own, down, up, far):
        for i in range(2):
            own[i] = k[i].astype(F32) + g[i].astype(F32)
            for n, out in enumerate((down, up, far)):
                at = 2 + 2 * n + i
                out[i] = (k[at].astype(F32) + g[at].astype(F32)).astype(BF)

    return _call(
        body,
        [_shape(2, tokens, 128, dtype=F32)] + [_shape(2, tokens, 128)] * 3,
        (keep, came),
    )


def scatter_y(down, up, far):
    return (
        _send(up, "tp", _ymove(1)),
        _send(down, "tp", _ymove(3)),
        _send(far, "tp", _ymove(2)),
    )


def scatter_two(own, below, above, far):
    def body(own, below, above, far, out):
        total = own[1] + below[1].astype(F32)
        out[0] = (total + above[1].astype(F32) + far[1].astype(F32)).astype(BF)

    return _call(body, [_shape(1, *own.shape[1:])], (own, below, above, far))[0]


def add_up(base, own, below, above, far, side, start=0):
    tokens = base.shape[0]

    def body(base, own, below, above, far, side, out):
        total = own[0] + below[0].astype(F32) + above[0].astype(F32)
        total = total + far[0].astype(F32)
        total = total + side[0, start : start + tokens, :].astype(F32)
        out[...] = (base[...].astype(F32) + total).astype(BF)

    return _call(
        body, [_shape(tokens, 128)], (base, own, below, above, far, side)
    )[0]


def outer_terms(me, lefts, rights, grads, parts):
    flat, plan = [], []

    def add(arrays):
        first = len(flat)
        flat.extend(arrays)
        return first, len(arrays)

    for left, right, grad in zip(lefts, rights, grads):
        plan.append(
            (
                add(left),
                right if isinstance(right, int) else add(right),
                add(grad),
            )
        )
    slots = lefts[0][0].shape[0]
    tokens = sum(a.shape[1] for a in lefts[0])
    rows = tokens // parts
    mats = len(plan) * 2 * slots
    n = len(flat)

    def body(me_ref, *refs):
        ins, (keep, send, held) = refs[:n], refs[n:]

        def read(entry, j, c):
            first, count = entry
            if count == parts:
                return ins[first + c][j]
            return ins[first][j, c * rows : c * rows + rows, :]

        def step(j, carry):
            for level, (left, right, grad) in enumerate(plan):
                total = None
                for c in range(parts):
                    if isinstance(right, int):
                        other = read(left, j ^ right, c)
                    else:
                        other = read(right, j, c)
                    both = _cat(read(left, j, c), other)
                    term = _dot_l(both, read(grad, j, c))
                    total = term if total is None else total + term
                held[...] = total
                for half in range(2):
                    mat = (level * 2 + half) * slots + j
                    for pos in range(16):
                        z0, xl, z1, z2 = pos >> 3, (pos >> 2) & 1, (pos >> 1) & 1, pos & 1
                        rel = xl * 8 + z2 * 4 + z1 * 2 + z0
                        row = half * 128 + (me_ref[0] ^ rel) * 8
                        value = held[pl.ds(pl.multiple_of(row, 8), 8), :]
                        if pos < 8:
                            keep[pos, mat] = value.astype(BF)
                        else:
                            send[pos - 8, mat] = value.astype(BF)
            return carry

        lax.fori_loop(0, slots, step, 0)

    return _call(
        body,
        [_shape(8, mats, 8, 128)] * 2,
        (me, *flat),
        scalars=1,
        scratch=[pltpu.VMEM((256, 128), F32)],
        flops=len(plan) * slots * tokens * 2 * 256 * 128,
    )


def halve(keeps, cames):
    n = len(keeps)
    size = keeps[0].shape[0] // 2
    mats = [k.shape[1] for k in keeps]

    def body(*refs):
        new_keep, new_send = refs[2 * n :]
        at = 0
        for k, c, m in zip(refs[:n], refs[n : 2 * n], mats):
            new_keep[:, at : at + m] = k[:size].astype(F32) + c[:size].astype(F32)
            new_send[:, at : at + m] = (
                k[size:].astype(F32) + c[size:].astype(F32)
            ).astype(BF)
            at += m

    total = sum(mats)
    return _call(
        body,
        [_shape(size, total, 8, 128, dtype=F32), _shape(size, total, 8, 128)],
        (*keeps, *cames),
    )


def last_half(keep, came, slots, scale):
    levels = keep.shape[1] // (2 * slots)

    def body(k, c, own, cross):
        for level in range(levels):
            for half, out in enumerate((own, cross)):
                at = (level * 2 + half) * slots
                rows = slice(at, at + slots)
                out[level] = (k[0, rows] + c[0, rows].astype(F32)) * scale

    return _call(body, [_shape(levels, slots, 8, 128, dtype=F32)] * 2, (keep, came))


def _mask(shape):
    row = lax.broadcasted_iota(jnp.int32, shape, 0)
    col = lax.broadcasted_iota(jnp.int32, shape, 1)
    return ((row ^ col) & 31) == 0


def _pick(shape):
    row = lax.broadcasted_iota(jnp.int32, shape, 0)
    col = lax.broadcasted_iota(jnp.int32, shape, 1)
    return (col >> 5) == row


def mix(factor, rows):
    def body(f, r, out):
        n, groups = f.shape
        wide = _dot(f[...], _pick((groups, n)).astype(BF))
        wide = jnp.where(_mask((n, n)), wide, 0.0).astype(BF)
        out[...] = _dot(wide, r[...]).astype(BF)

    return _call(
        body, [_shape(*rows.shape)], (factor, rows), flops=2 * 512 * 512 * 128
    )[0]


def second_terms(grads, rows):
    def body(g, r, out):
        n = r.shape[0]
        both = _dot_t(r[...], g[...])
        both = jnp.where(_mask((n, n)), both, 0.0)
        small = lax.dot_general(
            _pick((16, n)).astype(F32),
            both,
            (((1,), (0,)), ((), ())),
            precision=lax.Precision.HIGHEST,
            preferred_element_type=F32,
        )
        for k in range(4):
            out[k * 16 : k * 16 + 16, :] = small[:, k * 128 : k * 128 + 128].astype(BF)

    return _call(body, [_shape(64, 128)], (grads, rows), flops=2 * 512 * 512 * 128)[0]


def first_grad(grads, tokens, so_far, scale):
    n = len(grads)
    size = 512

    def body(*refs):
        gs, ts = refs[:n], refs[n : 2 * n]
        out, small = refs[-2:]
        if so_far is None:
            out[...] = jnp.zeros_like(out)
            small[...] = jnp.zeros_like(small)
        else:
            out[...] = refs[2 * n][...]
            small[...] = refs[2 * n + 1][...]
        for g, t in zip(gs, ts):

            def step(i, carry, g=g, t=t):
                one, two = 2 * i, 2 * i + 1
                left = _cat(g[one, 0:size, :], g[two, 0:size, :])
                out[...] += _dot_t(left, _cat(t[one, 0:size, :], t[two, 0:size, :]))
                small[...] += g[one, size:, :].astype(F32) + g[two, size:, :].astype(F32)
                return carry

            lax.fori_loop(0, g.shape[0] // 2, step, 0)
        if so_far is not None:
            out[...] = out[...] * scale
            small[...] = small[...] * scale

    more = () if so_far is None else tuple(so_far)
    return _call(
        body,
        [_shape(size, size, dtype=F32), _shape(64, 128, dtype=F32)],
        (*grads, *tokens, *more),
        flops=2 * size * size * 1024,
    )


def carry_rows(grad, extra, ride):
    tall = grad.shape[0] + extra.shape[0] + ride.shape[1]

    def body(g, e, r, out):
        n, m = g.shape[0], e.shape[0]
        out[0, 0:n, :] = g[...]
        out[0, n : n + m, :] = e[...]
        out[0, n + m :, :] = r[0]

    return _call(body, [_shape(1, tall, 128)], (grad, extra, ride))[0]


def split_rows(sent, side, rows):
    def body(s, x, pair):
        pair[0] = s[0, 0:rows, :]
        pair[1] = x[0, 0:rows, :]

    return _call(body, [_shape(2, rows, 128)], (sent, side))[0]


def per_device(
    tokens, w_first, second_factor, w_up, w_self, w_cross, w_down, block_pairs, cotangent
):
    seq_len, width = tokens.shape
    levels, slots = w_self.shape[:2]
    token_scale = 1.0 / math.sqrt(seq_len * lax.axis_size("seq"))
    width_scale = 1.0 / math.sqrt(width * lax.axis_size("tp"))
    parts = 2
    chunks = range(parts)
    me = lax.axis_index("seq").astype(jnp.int32).reshape(1)
    where = position(block_pairs.reshape(-1))
    factor = second_factor.transpose(1, 0, 2).reshape(512, 16)
    factor_t = second_factor.transpose(2, 0, 1).reshape(512, 16)
    partner_of = [None, None] + [_xor(1 << b) for b in range(levels - 2)]
    top = levels - 1

    def swap_seq(rows):
        moved = lax.all_to_all(
            rows.reshape(16, 32, 128), "seq", split_axis=0, concat_axis=0, tiled=True
        )
        return moved.reshape(512, 128)

    first_out = jnp.dot(w_first[0], tokens, preferred_element_type=F32).astype(BF)
    first_rows = swap_seq(first_out)
    early_block = jnp.concatenate([tokens, cotangent], 0)[None]
    early_block = after(early_block, first_out)
    early_side = _send(early_block, "tp", XHI)
    early_pair = join(early_block, early_side)
    mixed = mix(factor, after(first_rows, early_pair, me, where))
    early_y = gather_y(after(early_pair, mixed))
    mixed = after(swap_seq(mixed), early_y)
    hidden = (tokens.astype(F32) + mixed.astype(F32)).astype(BF)

    block = hidden[None]
    side = _send(block, "tp", XHI)
    pair = join(block, side)
    pair_y = gather_y(pair)
    blocks = gather_core(pair, *pair_y)
    early = gather_core(early_pair, *after(early_y, blocks))
    s0, s1, s2 = up_levels(where, blocks, w_up, w_self, w_cross)
    partner2 = _send(s2, "tp", partner_of[2])
    states, partners, grads = {}, {}, {}
    states[3] = level_up(s2, partner2, w_self, w_cross, 2, parts)
    grad_act = gather_grad(where, early, w_down, seq_len, parts)
    for level in range(3, levels):
        partners[level] = [_send(s, "tp", partner_of[level]) for s in states[level]]
        if level < top:
            states[level + 1] = [
                level_up(s, p, w_self, w_cross, level)[0]
                for s, p in zip(states[level], partners[level])
            ]
    acts, incoming = [None] * parts, [None] * parts
    grads[levels] = [None] * parts
    for c in chunks:
        acts[c], grads[levels][c], across = top_level(
            states[top][c], partners[top][c], w_self, w_cross, grad_act[c], top
        )
        incoming[c] = _send(across, "tp", partner_of[top])
    down_keep, down_send = down_pieces(where, acts, w_down)
    down_came = _send(down_send, "tp", CORE)
    for level in range(top, 2, -1):
        grads[level] = [None] * parts
        if level == 4:
            incoming[0] = after(incoming[0], down_send)
        if level == 3:
            upper = [3, 4, 5]
            upper_keep, upper_send = outer_terms(
                me,
                [states[l] for l in upper],
                [partners[l] for l in upper],
                [grads[l + 1] for l in upper],
                parts,
            )
            incoming[1] = after(incoming[1], upper_send)
        for c in chunks:
            grads[level][c], across = level_down(
                grads[level + 1][c], incoming[c], w_self, w_cross, level
            )
            incoming[c] = _send(across, "tp", partner_of[level - 1])
    upper_came = _send(upper_send, "seq", _xor(1))
    down_own, down_down, down_up, down_far = scatter_one(down_keep, down_came)
    grads[2], grads[1], keep, send = bottom_levels(
        where, grads[3], incoming, w_self, w_cross, w_up
    )
    came = _send(send, "tp", CORE)
    own, down, up, far = scatter_one(keep, came)
    below, above, far = scatter_y(down, up, far)
    lower_keep, lower_send = outer_terms(
        me, [[s0], [s1], [s2]], [1, 2, [partner2]], [[grads[1]], [grads[2]], grads[3]], parts
    )
    far = after(far, lower_send, upper_came)
    side = _send(scatter_two(own, below, above, far), "tp", XHI)
    lower_came = _send(lower_send, "seq", _xor(1))
    side = after(side, down_own)
    grad_hidden = add_up(cotangent, own, below, above, far, side)

    grad_rows = swap_seq(grad_hidden)
    down_below, down_above, down_far = scatter_y(
        *after((down_down, down_up, down_far), grad_hidden)
    )
    moved_back = mix(factor_t, after(grad_rows, lower_came))
    weights_keep, weights_send = halve(
        (lower_keep, upper_keep), (lower_came, upper_came)
    )
    weights_came = _send(weights_send, "seq", _xor(8))
    grad_first_out = swap_seq(moved_back)
    extra = second_terms(grad_rows, first_rows)
    ride = scatter_two(down_own, down_below, down_above, down_far)
    grad_first_out = after(grad_first_out, extra, ride, weights_came)
    side_block = carry_rows(grad_first_out, extra, ride)
    side = _send(side_block, "tp", XHI)
    weights_keep, weights_send = halve((weights_keep,), (weights_came,))
    weights_came = _send(weights_send, "seq", _xor(2))
    tall = 576
    pair = split_rows(side_block, side, tall)
    pair_y = gather_y(pair)
    weights_keep, weights_send = halve((weights_keep,), (weights_came,))
    weights_came = _send(weights_send, "seq", _xor(4))
    grad_mix = lax.dot_general(
        w_first[0], grad_first_out, (((0,), (0,)), ((), ())), preferred_element_type=F32
    )
    grad_tokens = (grad_hidden.astype(F32) + grad_mix).astype(BF)
    layer_out = add_up(
        hidden, down_own, down_below, down_above, down_far, side, start=tall
    )
    pair_y = after(pair_y, grad_tokens, layer_out, weights_came)
    late = gather_core(pair, *pair_y)
    grad_self, grad_cross = last_half(weights_keep, weights_came, slots, token_scale)

    half = first_grad(late[:1], early[:1], None, width_scale)
    grad_first, small = first_grad(late[1:], early[1:], half, width_scale)
    grad_second = (
        small.reshape(4, 16, 4, 32).transpose(3, 0, 2, 1).reshape(32, 16, 16)
    )
    return layer_out, grad_tokens, grad_first[None], grad_second, grad_self, grad_cross


def solution(mesh):
    in_specs = (
        P("seq", "tp"),
        P("seq", None, None),
        P("seq", None, None),
        P("tp", None, None, None),
        P(None, "tp", None, None),
        P(None, "tp", None, None),
        P("tp", None, None, None),
        P("tp", None),
        P("seq", "tp"),
    )
    out_specs = (
        P("seq", "tp"),
        P("seq", "tp"),
        P("seq", None, None),
        P("seq", None, None),
        P(None, "tp", "seq", None),
        P(None, "tp", "seq", None),
    )
    return jax.shard_map(
        per_device, mesh=mesh, in_specs=in_specs, out_specs=out_specs, check_vma=False
    )
```

```python
import math

import jax
import jax.numpy as jnp
from jax import lax
from jax.experimental import pallas as pl
from jax.experimental.pallas import tpu as pltpu
from jax.sharding import PartitionSpec as P


BF = jnp.bfloat16
F32 = jnp.float32
MIB = 1 << 20
ROOT = math.sqrt(2.0 / math.pi)


def _send(value, axis, target):
    return lax.ppermute(value, axis, [(s, target(s)) for s in range(16)])


def _xor(mask):
    return lambda t: t ^ mask


def _ymove(step):
    return lambda t: (t & 9) | (((((t >> 1) & 3) + step) & 3) << 1)


CORE, XHI = _xor(1), _xor(8)


def after(value, *others):
    return lax.optimization_barrier((value, others))[0]


def position(block):
    me = lax.axis_index("tp")
    dx = ((block ^ me) >> 3) & 1
    dc = (block ^ me) & 1
    dy = ((block >> 1) - (me >> 1)) & 3
    key = dx * 4 + dy
    order = jnp.zeros_like(key)
    for k, at in enumerate((0, 4, 6, 2, 1, 5, 7, 3)):
        order = order + jnp.where(key == k, at, 0)
    return (order + 8 * dc).astype(jnp.int32)


def _shape(*shape, dtype=BF):
    return jax.ShapeDtypeStruct(shape, dtype)


VMEM = pl.BlockSpec(memory_space=pltpu.VMEM)
SMEM = pl.BlockSpec(memory_space=pltpu.SMEM)


def _call(body, outs, args, scalars=0, scratch=(), flops=0, limit=8):
    moved = sum(a.size * a.dtype.itemsize for a in args) + sum(
        math.prod(o.shape) * o.dtype.itemsize for o in outs
    )
    return pl.pallas_call(
        body,
        in_specs=[SMEM] * scalars + [VMEM] * (len(args) - scalars),
        out_specs=[VMEM] * len(outs),
        out_shape=list(outs),
        scratch_shapes=list(scratch),
        compiler_params=pltpu.CompilerParams(vmem_limit_bytes=limit * MIB),
        cost_estimate=pl.CostEstimate(
            flops=flops, bytes_accessed=moved, transcendentals=0
        ),
    )(*args)


def _dot(a, b):
    return lax.dot_general(a, b, (((1,), (0,)), ((), ())), preferred_element_type=F32)


def _dot_t(a, b):
    return lax.dot_general(a, b, (((1,), (1,)), ((), ())), preferred_element_type=F32)


def _dot_l(a, b):
    return lax.dot_general(a, b, (((0,), (0,)), ((), ())), preferred_element_type=F32)


def _cat(a, b):
    return jnp.concatenate([a, b], axis=1)


def _stack(a, b):
    return jnp.concatenate([a, b], axis=0)


def join(*pieces, start=0):
    total = sum(p.shape[0] for p in pieces)
    rows = pieces[0].shape[1] - start

    def body(*refs):
        at = 0
        for ref in refs[:-1]:
            for i in range(ref.shape[0]):
                refs[-1][at] = ref[i, start:, :]
                at += 1

    return _call(body, [_shape(total, rows, 128)], pieces)[0]


def gather_y(pair):
    return (
        _send(pair, "tp", _ymove(1)),
        _send(pair, "tp", _ymove(3)),
        _send(pair, "tp", _ymove(2)),
    )


def gather_core(*pieces, start=0):
    own = join(*pieces, start=start)
    return own, _send(own, "tp", CORE)


def _hold(refs, held, start, rows):
    at = 0
    for ref in refs:
        for i in range(ref.shape[0]):
            held[at] = ref[i, start : start + rows, :]
            at += 1


def up_levels(where, blocks, w_up, w_self, w_cross):
    slots, tokens = w_up.shape[0], blocks[0].shape[1]
    n = len(blocks)

    def body(where_ref, *refs):
        ins, (up, ws, wc, s0, s1, s2, held) = refs[:n], refs[n:]
        _hold(ins, held, 0, tokens)

        def start(j, carry):
            left, right = held[where_ref[2 * j]], held[where_ref[2 * j + 1]]
            s0[j] = _dot(_cat(left, right), _stack(up[j, 0], up[j, 1])).astype(BF)
            return carry

        lax.fori_loop(0, slots, start, 0)
        for level, (src, dst) in enumerate(((s0, s1), (s1, s2))):

            def step(j, carry, level=level, src=src, dst=dst):
                both = _cat(src[j], src[j ^ (1 << level)])
                dst[j] = _dot(both, _stack(ws[level, j], wc[level, j])).astype(BF)
                return carry

            lax.fori_loop(0, slots, step, 0)

    return _call(
        body,
        [_shape(slots, tokens, 128)] * 3,
        (where, *blocks, w_up, w_self, w_cross),
        scalars=1,
        scratch=[pltpu.VMEM((16, tokens, 128), BF)],
        flops=3 * slots * tokens * 2 * 256 * 128,
    )


def split_weights(w_self, w_cross):
    levels, slots = w_self.shape[:2]

    def body(ws, wc, *outs):
        for n, out in enumerate(outs):

            def step(j, carry, n=n, out=out):
                out[j, 0:128, :] = ws[n + 2, j]
                out[j, 128:256, :] = wc[n + 2, j]
                return carry

            lax.fori_loop(0, slots, step, 0)

    outs = [_shape(slots, 256, 128)] * (levels - 2)
    return [None, None, *_call(body, outs, (w_self, w_cross))]


def level_up(state, partner, weight, parts=1):
    slots, tokens, _ = state.shape
    rows = tokens // parts

    def body(s, p, w, *outs):
        for c, out in enumerate(outs):
            at = slice(c * rows, c * rows + rows)
            for j in range(slots):
                out[j] = _dot(_cat(s[j, at, :], p[j, at, :]), w[j]).astype(BF)

    return _call(
        body,
        [_shape(slots, rows, 128)] * parts,
        (state, partner, weight),
        flops=slots * tokens * 2 * 256 * 128,
    )


def gather_grad(where, blocks, w_down, parts):
    slots = w_down.shape[0]
    tokens = blocks[0].shape[1]
    rows = tokens // parts
    n = len(blocks)

    def body(where_ref, *refs):
        ins, down, outs, held = refs[:n], refs[n], refs[n + 1 : -1], refs[-1]
        _hold(ins, held, 0, tokens)

        def step(j, carry):
            left, right = held[where_ref[2 * j]], held[where_ref[2 * j + 1]]
            total = _dot_t(_cat(left, right), _cat(down[j, 0], down[j, 1]))
            for c, out in enumerate(outs):
                out[j] = total[c * rows : c * rows + rows]
            return carry

        lax.fori_loop(0, slots, step, 0)

    return _call(
        body,
        [_shape(slots, rows, 128, dtype=F32)] * parts,
        (where, *blocks, w_down),
        scalars=1,
        scratch=[pltpu.VMEM((16, tokens, 128), BF)],
        flops=slots * tokens * 4 * 128 * 128,
    )


def top_level(state, partner, weight, grad_act):
    slots, tokens, _ = state.shape

    def body(s, p, w, ga, act, grad, across):
        def step(j, carry):
            v = _dot(_cat(s[j], p[j]), w[j]).astype(BF).astype(F32)
            square = v * v
            t = jnp.tanh(ROOT * (v + 0.044715 * (v * square)))
            act[j] = (0.5 * v * (1.0 + t)).astype(BF)
            slope = 0.5 * (1.0 + t) + (0.5 * ROOT) * v * (1.0 - t * t) * (
                1.0 + (3 * 0.044715) * square
            )
            g = (ga[j] * slope).astype(BF)
            grad[j] = g
            across[j] = _dot_t(g, w[j, 128:256, :]).astype(BF)
            return carry

        lax.fori_loop(0, slots, step, 0)

    return _call(
        body,
        [_shape(*state.shape)] * 3,
        (state, partner, weight, grad_act),
        flops=slots * tokens * 3 * 2 * 128 * 128,
    )


def level_down(grad, incoming, weight, below):
    slots, tokens, _ = grad.shape

    def body(g, inc, w, wb, out, across):
        for j in range(slots):
            new = (_dot_t(g[j], w[j, 0:128, :]) + inc[j].astype(F32)).astype(BF)
            out[j] = new
            across[j] = _dot_t(new, wb[j, 128:256, :]).astype(BF)

    return _call(
        body,
        [_shape(*grad.shape)] * 2,
        (grad, incoming, weight, below),
        flops=slots * tokens * 2 * 2 * 128 * 128,
    )


def bottom_levels(where, grads, incoming, w_self, w_cross, w_up):
    parts = len(grads)
    slots, rows, _ = grads[0].shape
    tokens = rows * parts

    def body(where_ref, *refs):
        gs, incs = refs[:parts], refs[parts : 2 * parts]
        ws, wc, up, g2, g1, keep, send, g0, total = refs[2 * parts :]

        def first(j, carry):
            for c in range(parts):
                new = _dot_t(gs[c][j], ws[2, j]) + incs[c][j].astype(F32)
                g2[j, c * rows : c * rows + rows, :] = new.astype(BF)
            return carry

        lax.fori_loop(0, slots, first, 0)
        for level, (src, dst) in ((1, (g2, g1)), (0, (g1, g0))):

            def step(j, carry, level=level, src=src, dst=dst):
                other = j ^ (1 << level)
                both = _cat(src[j], src[other])
                weight = _cat(ws[level, j], wc[level, other])
                dst[j] = _dot_t(both, weight).astype(BF)
                return carry

            lax.fori_loop(0, slots, step, 0)
        _scatter(
            where_ref, lambda i: _dot_t(g0[i >> 1], up[i >> 1, i & 1]), slots, total, keep, send
        )

    return _call(
        body,
        [_shape(slots, tokens, 128)] * 2 + [_shape(8, tokens, 128)] * 2,
        (where, *grads, *incoming, w_self, w_cross, w_up),
        scalars=1,
        scratch=[
            pltpu.VMEM((slots, tokens, 128), BF),
            pltpu.VMEM((16, tokens, 128), F32),
        ],
        flops=slots * tokens * 7 * 2 * 128 * 128,
        limit=12,
    )


def _scatter(where_ref, piece, slots, total, keep, send):
    total[...] = jnp.zeros_like(total)

    def step(i, carry):
        at = where_ref[i]
        total[at] = total[at] + piece(i)
        return carry

    def finish(i, carry):
        keep[i] = total[i].astype(BF)
        send[i] = total[i + 8].astype(BF)
        return carry

    lax.fori_loop(0, 2 * slots, step, 0)
    lax.fori_loop(0, 8, finish, 0)


def down_pieces(where, acts, w_down):
    parts = len(acts)
    slots, rows, _ = acts[0].shape
    tokens = rows * parts

    def body(where_ref, *refs):
        ins, (down, keep, send, total) = refs[:parts], refs[parts:]

        def piece(i):
            whole = jnp.concatenate([r[i >> 1] for r in ins], axis=0)
            return _dot(whole, down[i >> 1, i & 1])

        _scatter(where_ref, piece, slots, total, keep, send)

    return _call(
        body,
        [_shape(8, tokens, 128)] * 2,
        (where, *acts, w_down),
        scalars=1,
        scratch=[pltpu.VMEM((16, tokens, 128), F32)],
        flops=slots * tokens * 2 * 2 * 128 * 128,
        limit=12,
    )


def scatter_one(keep, came):
    tokens = keep.shape[1]

    def body(k, g, own, down, up, far):
        for i in range(2):
            own[i] = k[i].astype(F32) + g[i].astype(F32)
            for n, out in enumerate((down, up, far)):
                at = 2 + 2 * n + i
                out[i] = (k[at].astype(F32) + g[at].astype(F32)).astype(BF)

    return _call(
        body,
        [_shape(2, tokens, 128, dtype=F32)] + [_shape(2, tokens, 128)] * 3,
        (keep, came),
    )


def scatter_y(down, up, far):
    below = _send(up, "tp", _ymove(1))
    above = _send(down, "tp", _ymove(3))
    beyond = _send(far, "tp", _ymove(2))
    return below, above, beyond


def scatter_two(own, below, above, far):
    def body(own, below, above, far, out):
        total = own[1] + below[1].astype(F32)
        out[0] = (total + above[1].astype(F32) + far[1].astype(F32)).astype(BF)

    return _call(body, [_shape(1, *own.shape[1:])], (own, below, above, far))[0]


def add_up(base, own, below, above, far, side, start=0):
    tokens = base.shape[0]

    def body(base, own, below, above, far, side, out):
        total = own[0] + below[0].astype(F32) + above[0].astype(F32)
        total = total + far[0].astype(F32)
        total = total + side[0, start : start + tokens, :].astype(F32)
        out[...] = (base[...].astype(F32) + total).astype(BF)

    return _call(
        body, [_shape(tokens, 128)], (base, own, below, above, far, side)
    )[0]


def outer_terms(me, lefts, rights, grads, parts, more=()):
    flat, plan = [], []

    def add(arrays):
        first = len(flat)
        flat.extend(arrays)
        return first, len(arrays)

    for left, right, grad in zip(lefts, rights, grads):
        plan.append(
            (
                add(left),
                right if isinstance(right, int) else add(right),
                add(grad),
            )
        )
    slots = lefts[0][0].shape[0]
    tokens = sum(a.shape[1] for a in lefts[0])
    rows = tokens // parts
    mats = len(plan) * 2 * slots
    total_mats = mats + (more[0].shape[1] if more else 0)
    n = len(flat)

    def body(me_ref, *refs):
        ins, (keep, send, held) = refs[:n], refs[-3:]
        for old, new in zip(refs[n:-3], (keep, send)):

            def copy(pos, carry, old=old, new=new):
                new[pos, mats:] = old[pos]
                return carry

            lax.fori_loop(0, 8, copy, 0)

        def read(entry, j, c):
            first, count = entry
            if count == parts:
                return ins[first + c][j]
            return ins[first][j, c * rows : c * rows + rows, :]

        def step(j, carry):
            for level, (left, right, grad) in enumerate(plan):
                total = None
                for c in range(parts):
                    if isinstance(right, int):
                        other = read(left, j ^ right, c)
                    else:
                        other = read(right, j, c)
                    both = _cat(read(left, j, c), other)
                    term = _dot_l(both, read(grad, j, c))
                    total = term if total is None else total + term
                held[...] = total
                for half in range(2):
                    mat = (level * 2 + half) * slots + j
                    for pos in range(16):
                        z0, xl, z1, z2 = pos >> 3, (pos >> 2) & 1, (pos >> 1) & 1, pos & 1
                        rel = xl * 8 + z2 * 4 + z1 * 2 + z0
                        row = half * 128 + (me_ref[0] ^ rel) * 8
                        value = held[pl.ds(pl.multiple_of(row, 8), 8), :]
                        if pos < 8:
                            keep[pos, mat] = value.astype(BF)
                        else:
                            send[pos - 8, mat] = value.astype(BF)
            return carry

        lax.fori_loop(0, slots, step, 0)

    return _call(
        body,
        [_shape(8, total_mats, 8, 128)] * 2,
        (me, *flat, *more),
        scalars=1,
        scratch=[pltpu.VMEM((256, 128), F32)],
        flops=len(plan) * slots * tokens * 2 * 256 * 128,
    )


def halve(keeps, cames):
    n = len(keeps)
    size = keeps[0].shape[0] // 2
    mats = [k.shape[1] for k in keeps]

    def body(*refs):
        new_keep, new_send = refs[2 * n :]
        at = 0
        for k, c, m in zip(refs[:n], refs[n : 2 * n], mats):
            new_keep[:, at : at + m] = k[:size].astype(F32) + c[:size].astype(F32)
            new_send[:, at : at + m] = (
                k[size:].astype(F32) + c[size:].astype(F32)
            ).astype(BF)
            at += m

    total = sum(mats)
    return _call(
        body,
        [_shape(size, total, 8, 128, dtype=F32), _shape(size, total, 8, 128)],
        (*keeps, *cames),
    )


def last_half(keep, came, slots, scale):
    levels = keep.shape[1] // (2 * slots)

    def body(k, c, own, cross):
        for level in range(levels):
            for half, out in enumerate((own, cross)):
                at = (level * 2 + half) * slots
                rows = slice(at, at + slots)
                out[level] = (k[0, rows] + c[0, rows].astype(F32)) * scale

    return _call(body, [_shape(levels, slots, 8, 128, dtype=F32)] * 2, (keep, came))


def _mask(shape):
    row = lax.broadcasted_iota(jnp.int32, shape, 0)
    col = lax.broadcasted_iota(jnp.int32, shape, 1)
    return ((row ^ col) & 31) == 0


def _pick(shape):
    row = lax.broadcasted_iota(jnp.int32, shape, 0)
    col = lax.broadcasted_iota(jnp.int32, shape, 1)
    return (col >> 5) == row


def mix(factor, rows):
    def body(f, r, out):
        n, groups = f.shape

        def step(k, carry):
            at = pl.ds(pl.multiple_of(k * 256, 256), 256)
            wide = _dot(f[at, :], _pick((groups, n)).astype(BF))
            wide = jnp.where(_mask((256, n)), wide, 0.0).astype(BF)
            out[at, :] = _dot(wide, r[...]).astype(BF)
            return carry

        lax.fori_loop(0, n // 256, step, 0)

    return _call(
        body, [_shape(*rows.shape)], (factor, rows), flops=2 * 512 * 512 * 128
    )[0]


def second_terms(grads, rows):
    def body(g, r, out):
        n = r.shape[0]
        pick = _pick((16, n)).astype(BF)

        def step(k, carry):
            both = _dot_t(r[...], g[pl.ds(pl.multiple_of(k * 128, 128), 128), :])
            both = jnp.where(_mask((n, 128)), both, 0.0)
            high = both.astype(BF)
            low = (both - high.astype(F32)).astype(BF)
            small = _dot(pick, high) + _dot(pick, low)
            out[pl.ds(pl.multiple_of(k * 16, 16), 16), :] = small.astype(BF)
            return carry

        lax.fori_loop(0, 4, step, 0)

    return _call(body, [_shape(64, 128)], (grads, rows), flops=2 * 512 * 512 * 128)[0]


def first_grad(grads, tokens):
    n = len(grads)
    size = 512

    def body(*refs):
        gs, ts, (keep, send) = refs[:n], refs[n : 2 * n], refs[2 * n :]
        total, extra = None, None
        for g, t in zip(gs, ts):
            left = _cat(g[0, 0:size, :], g[1, 0:size, :])
            term = _dot_t(left, _cat(t[0, 0:size, :], t[1, 0:size, :]))
            more = g[0, size:, :].astype(F32) + g[1, size:, :].astype(F32)
            if total is None:
                keep[0:size] = term
            else:
                keep[0:size] = keep[0:size] + term
            total = term
            extra = more if extra is None else extra + more
        for k in range(4):
            lanes = slice(k * 128, k * 128 + 128)
            keep[size:, lanes] = extra[k * 16 : k * 16 + 16]
        send[...] = keep[...].astype(BF)

    return _call(
        body,
        [_shape(size + 16, size, dtype=F32), _shape(size + 16, size)],
        (*grads, *tokens),
        flops=2 * size * size * 1024,
    )


def finish_first(keep, came, scale):
    size = keep.shape[1]

    def body(k, c, out, small):
        out[...] = (k[0:size] + c[0:size].astype(F32)) * scale
        small[...] = (k[size:] + c[size:].astype(F32)) * scale

    return _call(
        body,
        [_shape(size, size, dtype=F32), _shape(16, size, dtype=F32)],
        (keep, came),
    )


def carry_rows(grad, extra, ride):
    tall = grad.shape[0] + extra.shape[0] + ride.shape[1]

    def body(g, e, r, out):
        n, m = g.shape[0], e.shape[0]
        out[0, 0:n, :] = g[...]
        out[0, n : n + m, :] = e[...]
        out[0, n + m :, :] = r[0]

    return _call(body, [_shape(1, tall, 128)], (grad, extra, ride))[0]


def split_rows(sent, side, rows):
    def body(s, x, pair):
        pair[0] = s[0, 0:rows, :]
        pair[1] = x[0, 0:rows, :]

    return _call(body, [_shape(2, rows, 128)], (sent, side))[0]


def layer(
    tokens, w_first, second_factor, w_up, w_self, w_cross, w_down, block_pairs, cotangent
):
    seq_len, width = tokens.shape
    levels, slots = w_self.shape[:2]
    token_scale = 1.0 / math.sqrt(seq_len * lax.axis_size("seq"))
    width_scale = 1.0 / math.sqrt(width * lax.axis_size("tp"))
    parts = 2
    chunks = range(parts)
    me = lax.axis_index("seq").astype(jnp.int32).reshape(1)
    where = position(block_pairs.reshape(-1))
    factor = second_factor.transpose(1, 0, 2).reshape(512, 16)
    factor_t = second_factor.transpose(2, 0, 1).reshape(512, 16)
    partner_of = [None, None] + [_xor(1 << b) for b in range(levels - 2)]
    top = levels - 1

    weights = split_weights(w_self, w_cross)

    def swap_seq(rows):
        moved = lax.all_to_all(
            rows.reshape(16, 32, 128), "seq", split_axis=0, concat_axis=0, tiled=True
        )
        return moved.reshape(512, 128)

    first_out = jnp.dot(w_first[0], tokens, preferred_element_type=F32).astype(BF)
    first_rows = swap_seq(first_out)
    early_block = jnp.concatenate([tokens, cotangent], 0)[None]
    early_block = after(early_block, first_out)
    early_side = _send(early_block, "tp", XHI)
    early_pair = join(early_block, early_side)
    early_y = gather_y(early_pair)
    mixed = mix(factor, after(first_rows, early_pair, me, where, factor_t, weights))
    mixed = after(swap_seq(mixed), early_y)
    hidden = (tokens.astype(F32) + mixed.astype(F32)).astype(BF)

    block = hidden[None]
    side = _send(block, "tp", XHI)
    pair = join(block, side)
    pair_y = gather_y(pair)
    blocks = gather_core(pair, *pair_y)
    early = gather_core(early_pair, *after(early_y, blocks), start=seq_len)
    s0, s1, s2 = up_levels(where, blocks, w_up, w_self, w_cross)
    partner2 = _send(s2, "tp", partner_of[2])
    states, partners, grads = {}, {}, {}
    states[3] = level_up(s2, partner2, weights[2], parts)
    grad_act = gather_grad(where, early, w_down, parts)
    for level in range(3, levels):
        partners[level] = [_send(s, "tp", partner_of[level]) for s in states[level]]
        if level < top:
            states[level + 1] = [
                level_up(s, p, weights[level])[0]
                for s, p in zip(states[level], partners[level])
            ]
    acts, incoming = [None] * parts, [None] * parts
    grads[levels] = [None] * parts
    for c in chunks:
        acts[c], grads[levels][c], across = top_level(
            states[top][c], partners[top][c], weights[top], grad_act[c]
        )
        incoming[c] = _send(across, "tp", partner_of[top])
    down_keep, down_send = down_pieces(where, acts, w_down)
    down_came = _send(down_send, "tp", CORE)
    for level in range(top, 2, -1):
        grads[level] = [None] * parts
        if level == 4:
            incoming[0] = after(incoming[0], down_send)
        if level == 3:
            upper = [3, 4, 5]
            upper_keep, upper_send = outer_terms(
                me,
                [states[l] for l in upper],
                [partners[l] for l in upper],
                [grads[l + 1] for l in upper],
                parts,
            )
            incoming[1] = after(incoming[1], upper_send)
        for c in chunks:
            grads[level][c], across = level_down(
                grads[level + 1][c], incoming[c], weights[level], weights[level - 1]
            )
            incoming[c] = _send(across, "tp", partner_of[level - 1])
    down_own, down_down, down_up, down_far = scatter_one(down_keep, down_came)
    grads[2], grads[1], keep, send = bottom_levels(
        where, grads[3], incoming, w_self, w_cross, w_up
    )
    came = _send(send, "tp", CORE)
    own, down, up, far = scatter_one(keep, came)
    below, above, far = scatter_y(down, up, far)
    grads[1], grads[2] = after((grads[1], grads[2]), own)
    weights_keep, weights_send = outer_terms(
        me, [[s0], [s1], [s2]], [1, 2, [partner2]], [[grads[1]], [grads[2]], grads[3]], parts,
        (upper_keep, upper_send),
    )
    weights_came = _send(weights_send, "seq", _xor(1))
    far = after(far, weights_send)
    side = _send(scatter_two(own, below, above, far), "tp", XHI)
    side = after(side, down_own)
    grad_hidden = add_up(cotangent, own, below, above, far, side)

    grad_rows = swap_seq(grad_hidden)
    down_below, down_above, down_far = scatter_y(
        *after((down_down, down_up, down_far), grad_hidden)
    )
    moved_back = mix(factor_t, after(grad_rows, weights_came))
    weights_keep, weights_send = halve((weights_keep,), (weights_came,))
    weights_came = _send(weights_send, "seq", _xor(8))
    grad_first_out = swap_seq(moved_back)
    extra = second_terms(grad_rows, first_rows)
    ride = scatter_two(down_own, down_below, down_above, down_far)
    grad_first_out = after(grad_first_out, extra, ride, weights_came)
    side_block = carry_rows(grad_first_out, extra, ride)
    side = _send(side_block, "tp", XHI)
    weights_keep, weights_send = halve((weights_keep,), (weights_came,))
    weights_came = _send(weights_send, "seq", _xor(2))
    tall = 576
    pair = split_rows(side_block, side, tall)
    pair_y = gather_y(pair)
    weights_keep, weights_send = halve((weights_keep,), (weights_came,))
    weights_came = _send(weights_send, "seq", _xor(4))
    grad_mix = lax.dot_general(
        w_first[0], grad_first_out, (((0,), (0,)), ((), ())), preferred_element_type=F32
    )
    grad_tokens = (grad_hidden.astype(F32) + grad_mix).astype(BF)
    layer_out = add_up(
        hidden, down_own, down_below, down_above, down_far, side, start=tall
    )
    pair_y = after(pair_y, grad_tokens, layer_out, weights_came)
    first_keep, first_send = first_grad((pair, *pair_y), (early_pair, *early_y))
    first_came = _send(first_send, "tp", CORE)
    weights_keep = after(weights_keep, first_send)
    grad_self, grad_cross = last_half(weights_keep, weights_came, slots, token_scale)
    grad_first, small = finish_first(first_keep, first_came, width_scale)
    grad_second = small.reshape(16, 16, 32).transpose(2, 1, 0)
    return layer_out, grad_tokens, grad_first[None], grad_second, grad_self, grad_cross


def solution(mesh):
    in_specs = (
        P("seq", "tp"),
        P("seq", None, None),
        P("seq", None, None),
        P("tp", None, None, None),
        P(None, "tp", None, None),
        P(None, "tp", None, None),
        P("tp", None, None, None),
        P("tp", None),
        P("seq", "tp"),
    )
    out_specs = (
        P("seq", "tp"),
        P("seq", "tp"),
        P("seq", None, None),
        P("seq", None, None),
        P(None, "tp", "seq", None),
        P(None, "tp", "seq", None),
    )
    return jax.shard_map(
        layer, mesh=mesh, in_specs=in_specs, out_specs=out_specs, check_vma=False
    )
```

```python
import math

import jax
import jax.numpy as jnp
from jax import lax
from jax.experimental import pallas as pl
from jax.experimental.pallas import tpu as pltpu
from jax.sharding import PartitionSpec as P


BF = jnp.bfloat16
F32 = jnp.float32
MIB = 1 << 20
ROOT = math.sqrt(2.0 / math.pi)


def _send(value, axis, target):
    return lax.ppermute(value, axis, [(s, target(s)) for s in range(16)])


def _xor(mask):
    return lambda t: t ^ mask


def _ymove(step):
    return lambda t: (t & 9) | (((((t >> 1) & 3) + step) & 3) << 1)


CORE, XHI = _xor(1), _xor(8)


def after(value, *others):
    return lax.optimization_barrier((value, others))[0]


def position(block):
    me = lax.axis_index("tp")
    dx = ((block ^ me) >> 3) & 1
    dc = (block ^ me) & 1
    dy = ((block >> 1) - (me >> 1)) & 3
    key = dx * 4 + dy
    order = jnp.zeros_like(key)
    for k, at in enumerate((0, 4, 6, 2, 1, 5, 7, 3)):
        order = order + jnp.where(key == k, at, 0)
    return (order + 8 * dc).astype(jnp.int32)


def _shape(*shape, dtype=BF):
    return jax.ShapeDtypeStruct(shape, dtype)


VMEM = pl.BlockSpec(memory_space=pltpu.VMEM)
SMEM = pl.BlockSpec(memory_space=pltpu.SMEM)


def _call(body, outs, args, scalars=0, scratch=(), flops=0, limit=8):
    moved = sum(a.size * a.dtype.itemsize for a in args) + sum(
        math.prod(o.shape) * o.dtype.itemsize for o in outs
    )
    return pl.pallas_call(
        body,
        in_specs=[SMEM] * scalars + [VMEM] * (len(args) - scalars),
        out_specs=[VMEM] * len(outs),
        out_shape=list(outs),
        scratch_shapes=list(scratch),
        compiler_params=pltpu.CompilerParams(vmem_limit_bytes=limit * MIB),
        cost_estimate=pl.CostEstimate(
            flops=flops, bytes_accessed=moved, transcendentals=0
        ),
    )(*args)


def _dot(a, b):
    return lax.dot_general(a, b, (((1,), (0,)), ((), ())), preferred_element_type=F32)


def _dot_t(a, b):
    return lax.dot_general(a, b, (((1,), (1,)), ((), ())), preferred_element_type=F32)


def _dot_l(a, b):
    return lax.dot_general(a, b, (((0,), (0,)), ((), ())), preferred_element_type=F32)


def _cat(a, b):
    return jnp.concatenate([a, b], axis=1)


def _stack(a, b):
    return jnp.concatenate([a, b], axis=0)


def join(*pieces, start=0):
    total = sum(p.shape[0] for p in pieces)
    rows = pieces[0].shape[1] - start

    def body(*refs):
        at = 0
        for ref in refs[:-1]:
            for i in range(ref.shape[0]):
                refs[-1][at] = ref[i, start:, :]
                at += 1

    return _call(body, [_shape(total, rows, 128)], pieces)[0]


def gather_y(pair):
    below = _send(pair, "tp", _ymove(1))
    above = _send(pair, "tp", _ymove(3))
    far = _send(pair, "tp", _ymove(2))
    return below, above, far


def gather_core(*pieces, start=0):
    own = join(*pieces, start=start)
    return own, _send(own, "tp", CORE)


def _hold(refs, held, start, rows):
    at = 0
    for ref in refs:
        for i in range(ref.shape[0]):
            held[at] = ref[i, start : start + rows, :]
            at += 1


def up_levels(where, blocks, w_up, w_self, w_cross):
    slots, tokens = w_up.shape[0], blocks[0].shape[1]
    n = len(blocks)

    def body(where_ref, *refs):
        ins, (up, ws, wc, s0, s1, s2, held) = refs[:n], refs[n:]
        _hold(ins, held, 0, tokens)

        for j in range(slots):
            left, right = held[where_ref[2 * j]], held[where_ref[2 * j + 1]]
            s0[j] = _dot(_cat(left, right), _stack(up[j, 0], up[j, 1])).astype(BF)
        for level, (src, dst) in enumerate(((s0, s1), (s1, s2))):
            for j in range(slots):
                both = _cat(src[j], src[j ^ (1 << level)])
                dst[j] = _dot(both, _stack(ws[level, j], wc[level, j])).astype(BF)

    return _call(
        body,
        [_shape(slots, tokens, 128)] * 3,
        (where, *blocks, w_up, w_self, w_cross),
        scalars=1,
        scratch=[pltpu.VMEM((16, tokens, 128), BF)],
        flops=3 * slots * tokens * 2 * 256 * 128,
    )


def split_weights(w_self, w_cross):
    levels, slots = w_self.shape[:2]

    def body(ws, wc, *outs):
        for n, out in enumerate(outs):

            def step(j, carry, n=n, out=out):
                out[j, 0:128, :] = ws[n + 2, j]
                out[j, 128:256, :] = wc[n + 2, j]
                return carry

            lax.fori_loop(0, slots, step, 0)

    outs = [_shape(slots, 256, 128)] * (levels - 2)
    return [None, None, *_call(body, outs, (w_self, w_cross))]


def level_up(state, partner, weight, parts=1):
    slots, tokens, _ = state.shape
    rows = tokens // parts

    def body(s, p, w, *outs):
        for c, out in enumerate(outs):
            at = slice(c * rows, c * rows + rows)
            for j in range(slots):
                out[j] = _dot(_cat(s[j, at, :], p[j, at, :]), w[j]).astype(BF)

    return _call(
        body,
        [_shape(slots, rows, 128)] * parts,
        (state, partner, weight),
        flops=slots * tokens * 2 * 256 * 128,
    )


def gather_grad(where, blocks, w_down, parts):
    slots = w_down.shape[0]
    tokens = blocks[0].shape[1]
    rows = tokens // parts
    n = len(blocks)

    def body(where_ref, *refs):
        ins, down, outs, held = refs[:n], refs[n], refs[n + 1 : -1], refs[-1]
        _hold(ins, held, 0, tokens)

        def step(j, carry):
            left, right = held[where_ref[2 * j]], held[where_ref[2 * j + 1]]
            total = _dot_t(_cat(left, right), _cat(down[j, 0], down[j, 1]))
            for c, out in enumerate(outs):
                out[j] = total[c * rows : c * rows + rows]
            return carry

        lax.fori_loop(0, slots, step, 0)

    return _call(
        body,
        [_shape(slots, rows, 128, dtype=F32)] * parts,
        (where, *blocks, w_down),
        scalars=1,
        scratch=[pltpu.VMEM((16, tokens, 128), BF)],
        flops=slots * tokens * 4 * 128 * 128,
    )


def top_level(state, partner, weight, grad_act):
    slots, tokens, _ = state.shape

    def body(s, p, w, ga, act, grad, across):
        for j in range(slots):
            v = _dot(_cat(s[j], p[j]), w[j]).astype(BF).astype(F32)
            square = v * v
            t = jnp.tanh(ROOT * (v + 0.044715 * (v * square)))
            act[j] = (0.5 * v * (1.0 + t)).astype(BF)
            slope = 0.5 * (1.0 + t) + (0.5 * ROOT) * v * (1.0 - t * t) * (
                1.0 + (3 * 0.044715) * square
            )
            g = (ga[j] * slope).astype(BF)
            grad[j] = g
            across[j] = _dot_t(g, w[j, 128:256, :]).astype(BF)

    return _call(
        body,
        [_shape(*state.shape)] * 3,
        (state, partner, weight, grad_act),
        flops=slots * tokens * 3 * 2 * 128 * 128,
    )


def level_down(grad, incoming, weight, below):
    slots, tokens, _ = grad.shape

    def body(g, inc, w, wb, out, across):
        for j in range(slots):
            new = (_dot_t(g[j], w[j, 0:128, :]) + inc[j].astype(F32)).astype(BF)
            out[j] = new
            across[j] = _dot_t(new, wb[j, 128:256, :]).astype(BF)

    return _call(
        body,
        [_shape(*grad.shape)] * 2,
        (grad, incoming, weight, below),
        flops=slots * tokens * 2 * 2 * 128 * 128,
    )


def bottom_levels(where, grads, incoming, w_self, w_cross, w_up):
    parts = len(grads)
    slots, rows, _ = grads[0].shape
    tokens = rows * parts

    def body(where_ref, *refs):
        gs, incs = refs[:parts], refs[parts : 2 * parts]
        ws, wc, up, g2, g1, keep, send, g0, total = refs[2 * parts :]

        for c in range(parts):
            for j in range(slots):
                new = _dot_t(gs[c][j], ws[2, j]) + incs[c][j].astype(F32)
                g2[j, c * rows : c * rows + rows, :] = new.astype(BF)
        for level, (src, dst) in ((1, (g2, g1)), (0, (g1, g0))):
            for j in range(slots):
                other = j ^ (1 << level)
                both = _cat(src[j], src[other])
                weight = _cat(ws[level, j], wc[level, other])
                dst[j] = _dot_t(both, weight).astype(BF)
        total[...] = jnp.zeros_like(total)
        for j in range(slots):
            for k in range(2):
                at = where_ref[2 * j + k]
                total[at] = total[at] + _dot_t(g0[j], up[j, k])
        keep[...] = total[0:8].astype(BF)
        send[...] = total[8:16].astype(BF)

    return _call(
        body,
        [_shape(slots, tokens, 128)] * 2 + [_shape(8, tokens, 128)] * 2,
        (where, *grads, *incoming, w_self, w_cross, w_up),
        scalars=1,
        scratch=[
            pltpu.VMEM((slots, tokens, 128), BF),
            pltpu.VMEM((16, tokens, 128), F32),
        ],
        flops=slots * tokens * 7 * 2 * 128 * 128,
        limit=12,
    )


def _scatter(where_ref, piece, slots, total, keep, send):
    total[...] = jnp.zeros_like(total)

    def step(i, carry):
        at = where_ref[i]
        total[at] = total[at] + piece(i)
        return carry

    def finish(i, carry):
        keep[i] = total[i].astype(BF)
        send[i] = total[i + 8].astype(BF)
        return carry

    lax.fori_loop(0, 2 * slots, step, 0)
    lax.fori_loop(0, 8, finish, 0)


def down_pieces(where, acts, w_down):
    parts = len(acts)
    slots, rows, _ = acts[0].shape
    tokens = rows * parts

    def body(where_ref, *refs):
        ins, (down, keep, send, total) = refs[:parts], refs[parts:]

        def piece(i):
            whole = jnp.concatenate([r[i >> 1] for r in ins], axis=0)
            return _dot(whole, down[i >> 1, i & 1])

        _scatter(where_ref, piece, slots, total, keep, send)

    return _call(
        body,
        [_shape(8, tokens, 128)] * 2,
        (where, *acts, w_down),
        scalars=1,
        scratch=[pltpu.VMEM((16, tokens, 128), F32)],
        flops=slots * tokens * 2 * 2 * 128 * 128,
        limit=12,
    )


def scatter_one(keep, came):
    tokens = keep.shape[1]

    def body(k, g, own, down, up, far):
        for i in range(2):
            own[i] = k[i].astype(F32) + g[i].astype(F32)
            for n, out in enumerate((down, up, far)):
                at = 2 + 2 * n + i
                out[i] = (k[at].astype(F32) + g[at].astype(F32)).astype(BF)

    return _call(
        body,
        [_shape(2, tokens, 128, dtype=F32)] + [_shape(2, tokens, 128)] * 3,
        (keep, came),
    )


def scatter_y(down, up, far):
    below = _send(up, "tp", _ymove(1))
    above = _send(down, "tp", _ymove(3))
    beyond = _send(far, "tp", _ymove(2))
    return below, above, beyond


def scatter_two(own, below, above, far):
    def body(own, below, above, far, out):
        total = own[1] + below[1].astype(F32)
        out[0] = (total + above[1].astype(F32) + far[1].astype(F32)).astype(BF)

    return _call(body, [_shape(1, *own.shape[1:])], (own, below, above, far))[0]


def add_up(base, own, below, above, far, side, start=0):
    tokens = base.shape[0]

    def body(base, own, below, above, far, side, out):
        total = own[0] + below[0].astype(F32) + above[0].astype(F32)
        total = total + far[0].astype(F32)
        total = total + side[0, start : start + tokens, :].astype(F32)
        out[...] = (base[...].astype(F32) + total).astype(BF)

    return _call(
        body, [_shape(tokens, 128)], (base, own, below, above, far, side)
    )[0]


def outer_terms(me, lefts, rights, grads, parts, more=()):
    flat, plan = [], []

    def add(arrays):
        first = len(flat)
        flat.extend(arrays)
        return first, len(arrays)

    for left, right, grad in zip(lefts, rights, grads):
        plan.append(
            (
                add(left),
                right if isinstance(right, int) else add(right),
                add(grad),
            )
        )
    slots = lefts[0][0].shape[0]
    tokens = sum(a.shape[1] for a in lefts[0])
    rows = tokens // parts
    mats = len(plan) * 2 * slots
    total_mats = mats + (more[0].shape[1] if more else 0)
    n = len(flat)

    def body(me_ref, *refs):
        ins, (keep, send, held) = refs[:n], refs[-3:]
        for old, new in zip(refs[n:-3], (keep, send)):

            def copy(pos, carry, old=old, new=new):
                new[pos, mats:] = old[pos]
                return carry

            lax.fori_loop(0, 8, copy, 0)

        def read(entry, j, c):
            first, count = entry
            if count == parts:
                return ins[first + c][j]
            return ins[first][j, c * rows : c * rows + rows, :]

        def step(j, carry):
            for level, (left, right, grad) in enumerate(plan):
                total = None
                for c in range(parts):
                    if isinstance(right, int):
                        other = read(left, j ^ right, c)
                    else:
                        other = read(right, j, c)
                    both = _cat(read(left, j, c), other)
                    term = _dot_l(both, read(grad, j, c))
                    total = term if total is None else total + term
                held[...] = total
                for half in range(2):
                    mat = (level * 2 + half) * slots + j
                    for pos in range(16):
                        z0, xl, z1, z2 = pos >> 3, (pos >> 2) & 1, (pos >> 1) & 1, pos & 1
                        rel = xl * 8 + z2 * 4 + z1 * 2 + z0
                        row = half * 128 + (me_ref[0] ^ rel) * 8
                        value = held[pl.ds(pl.multiple_of(row, 8), 8), :]
                        if pos < 8:
                            keep[pos, mat] = value.astype(BF)
                        else:
                            send[pos - 8, mat] = value.astype(BF)
            return carry

        lax.fori_loop(0, slots, step, 0)

    return _call(
        body,
        [_shape(8, total_mats, 8, 128)] * 2,
        (me, *flat, *more),
        scalars=1,
        scratch=[pltpu.VMEM((256, 128), F32)],
        flops=len(plan) * slots * tokens * 2 * 256 * 128,
    )


def halve(keeps, cames):
    n = len(keeps)
    size = keeps[0].shape[0] // 2
    mats = [k.shape[1] for k in keeps]

    def body(*refs):
        new_keep, new_send = refs[2 * n :]
        at = 0
        for k, c, m in zip(refs[:n], refs[n : 2 * n], mats):
            new_keep[:, at : at + m] = k[:size].astype(F32) + c[:size].astype(F32)
            new_send[:, at : at + m] = (
                k[size:].astype(F32) + c[size:].astype(F32)
            ).astype(BF)
            at += m

    total = sum(mats)
    return _call(
        body,
        [_shape(size, total, 8, 128, dtype=F32), _shape(size, total, 8, 128)],
        (*keeps, *cames),
    )


HBM = pl.BlockSpec(memory_space=pltpu.HBM)


def halve_first(keeps, cames):
    n = len(keeps)
    size = keeps[0].shape[0] // 2
    mats = [k.shape[1] for k in keeps]
    args = (*keeps, *cames)

    def body(*refs):
        ins, (new_keep, new_send), held = refs[: 2 * n], refs[2 * n : 2 * n + 2], refs[2 * n + 2 : -1]
        copies = [
            pltpu.make_async_copy(ref, buf, refs[-1].at[i])
            for i, (ref, buf) in enumerate(zip(ins, held))
        ]
        for copy in copies:
            copy.start()
        for copy in copies:
            copy.wait()
        at = 0
        for k, c, m in zip(held[:n], held[n:], mats):
            new_keep[:, at : at + m] = k[:size].astype(F32) + c[:size].astype(F32)
            new_send[:, at : at + m] = (
                k[size:].astype(F32) + c[size:].astype(F32)
            ).astype(BF)
            at += m

    total = sum(mats)
    return pl.pallas_call(
        body,
        in_specs=[HBM] * len(args),
        out_specs=[VMEM] * 2,
        out_shape=[
            _shape(size, total, 8, 128, dtype=F32),
            _shape(size, total, 8, 128),
        ],
        scratch_shapes=[pltpu.VMEM(a.shape, a.dtype) for a in args]
        + [pltpu.SemaphoreType.DMA((len(args),))],
        compiler_params=pltpu.CompilerParams(vmem_limit_bytes=8 * MIB),
        cost_estimate=pl.CostEstimate(
            flops=0, bytes_accessed=4 * MIB, transcendentals=0
        ),
    )(*args)


def last_half(keep, came, slots, scale):
    levels = keep.shape[1] // (2 * slots)

    def body(k, c, own, cross):
        for level in range(levels):
            for half, out in enumerate((own, cross)):
                at = (level * 2 + half) * slots
                rows = slice(at, at + slots)
                out[level] = (k[0, rows] + c[0, rows].astype(F32)) * scale

    return _call(body, [_shape(levels, slots, 8, 128, dtype=F32)] * 2, (keep, came))


def _mask(shape):
    row = lax.broadcasted_iota(jnp.int32, shape, 0)
    col = lax.broadcasted_iota(jnp.int32, shape, 1)
    return ((row ^ col) & 31) == 0


def _pick(shape):
    row = lax.broadcasted_iota(jnp.int32, shape, 0)
    col = lax.broadcasted_iota(jnp.int32, shape, 1)
    return (col >> 5) == row


def mix(factor, rows):
    def body(f, r, out):
        n, groups = f.shape
        wide = _dot(f[...], _pick((groups, n)).astype(BF))
        wide = jnp.where(_mask((n, n)), wide, 0.0).astype(BF)
        out[...] = _dot(wide, r[...]).astype(BF)

    return _call(
        body, [_shape(*rows.shape)], (factor, rows), flops=2 * 512 * 512 * 128
    )[0]


def second_terms(grads, rows):
    def body(g, r, out):
        n = r.shape[0]
        pick = _pick((16, n)).astype(BF)

        def step(k, carry):
            both = _dot_t(r[...], g[pl.ds(pl.multiple_of(k * 128, 128), 128), :])
            both = jnp.where(_mask((n, 128)), both, 0.0)
            high = both.astype(BF)
            low = (both - high.astype(F32)).astype(BF)
            small = _dot(pick, high) + _dot(pick, low)
            out[pl.ds(pl.multiple_of(k * 16, 16), 16), :] = small.astype(BF)
            return carry

        lax.fori_loop(0, 4, step, 0)

    return _call(body, [_shape(64, 128)], (grads, rows), flops=2 * 512 * 512 * 128)[0]


def first_grad(grads, tokens):
    n = len(grads)
    size = 512

    def body(*refs):
        gs, ts, (keep, send) = refs[:n], refs[n : 2 * n], refs[2 * n :]
        wide = lambda refs: jnp.concatenate(
            [r[i, 0:size, :] for r in refs for i in range(2)], axis=1
        )
        term = _dot_t(wide(gs), wide(ts))
        keep[0:size] = term
        send[0:size] = term.astype(BF)
        extra = None
        for g in gs:
            more = g[0, size:, :].astype(F32) + g[1, size:, :].astype(F32)
            extra = more if extra is None else extra + more
        for k in range(4):
            lanes = slice(k * 128, k * 128 + 128)
            keep[size:, lanes] = extra[k * 16 : k * 16 + 16]
            send[size:, lanes] = extra[k * 16 : k * 16 + 16].astype(BF)

    return _call(
        body,
        [_shape(size + 16, size, dtype=F32), _shape(size + 16, size)],
        (*grads, *tokens),
        flops=2 * size * size * 1024,
    )


def finish_first(keep, came, scale):
    size = keep.shape[1]

    def body(k, c, out, small):
        out[...] = (k[0:size] + c[0:size].astype(F32)) * scale
        small[...] = (k[size:] + c[size:].astype(F32)) * scale

    return _call(
        body,
        [_shape(size, size, dtype=F32), _shape(16, size, dtype=F32)],
        (keep, came),
    )


def carry_rows(grad, extra, ride):
    tall = grad.shape[0] + extra.shape[0] + ride.shape[1]

    def body(g, e, r, out):
        n, m = g.shape[0], e.shape[0]
        out[0, 0:n, :] = g[...]
        out[0, n : n + m, :] = e[...]
        out[0, n + m :, :] = r[0]

    return _call(body, [_shape(1, tall, 128)], (grad, extra, ride))[0]


def split_rows(sent, side, rows):
    def body(s, x, pair):
        pair[0] = s[0, 0:rows, :]
        pair[1] = x[0, 0:rows, :]

    return _call(body, [_shape(2, rows, 128)], (sent, side))[0]


def layer(
    tokens, w_first, second_factor, w_up, w_self, w_cross, w_down, block_pairs, cotangent
):
    seq_len, width = tokens.shape
    levels, slots = w_self.shape[:2]
    token_scale = 1.0 / math.sqrt(seq_len * lax.axis_size("seq"))
    width_scale = 1.0 / math.sqrt(width * lax.axis_size("tp"))
    parts = 2
    chunks = range(parts)
    me = lax.axis_index("seq").astype(jnp.int32).reshape(1)
    where = position(block_pairs.reshape(-1))
    factor = second_factor.transpose(1, 0, 2).reshape(512, 16)
    factor_t = second_factor.transpose(2, 0, 1).reshape(512, 16)
    partner_of = [None, None] + [_xor(1 << b) for b in range(levels - 2)]
    top = levels - 1

    weights = split_weights(w_self, w_cross)

    def swap_seq(rows):
        moved = lax.all_to_all(
            rows.reshape(16, 32, 128), "seq", split_axis=0, concat_axis=0, tiled=True
        )
        return moved.reshape(512, 128)

    first_out = jnp.dot(w_first[0], tokens, preferred_element_type=F32).astype(BF)
    first_rows = swap_seq(first_out)
    early_block = jnp.concatenate([tokens, cotangent], 0)[None]
    early_block = after(early_block, first_out)
    early_side = _send(early_block, "tp", XHI)
    early_pair = join(early_block, early_side)
    early_y = gather_y(early_pair)
    mixed = mix(factor, after(first_rows, early_pair, me, where, factor_t, weights))
    mixed = after(swap_seq(mixed), early_y)
    hidden = (tokens.astype(F32) + mixed.astype(F32)).astype(BF)

    block = hidden[None]
    side = _send(block, "tp", XHI)
    pair = join(block, side)
    pair_y = gather_y(pair)
    blocks = gather_core(pair, *pair_y)
    early = gather_core(early_pair, *after(early_y, blocks), start=seq_len)
    s0, s1, s2 = up_levels(where, blocks, w_up, w_self, w_cross)
    partner2 = _send(s2, "tp", partner_of[2])
    states, partners, grads = {}, {}, {}
    states[3] = level_up(s2, partner2, weights[2], parts)
    grad_act = gather_grad(where, early, w_down, parts)
    for level in range(3, levels):
        partners[level] = [_send(s, "tp", partner_of[level]) for s in states[level]]
        if level < top:
            states[level + 1] = [
                level_up(s, p, weights[level])[0]
                for s, p in zip(states[level], partners[level])
            ]
    acts, incoming = [None] * parts, [None] * parts
    grads[levels] = [None] * parts
    for c in chunks:
        acts[c], grads[levels][c], across = top_level(
            states[top][c], partners[top][c], weights[top], grad_act[c]
        )
        incoming[c] = _send(across, "tp", partner_of[top])
    down_keep, down_send = down_pieces(where, acts, w_down)
    down_came = _send(down_send, "tp", CORE)
    for level in range(top, 2, -1):
        grads[level] = [None] * parts
        if level == 4:
            incoming[0] = after(incoming[0], down_send)
        if level == 3:
            upper = [3, 4, 5]
            upper_keep, upper_send = outer_terms(
                me,
                [states[l] for l in upper],
                [partners[l] for l in upper],
                [grads[l + 1] for l in upper],
                parts,
            )
            incoming[1] = after(incoming[1], upper_send)
        for c in chunks:
            grads[level][c], across = level_down(
                grads[level + 1][c], incoming[c], weights[level], weights[level - 1]
            )
            incoming[c] = _send(across, "tp", partner_of[level - 1])
    down_own, down_down, down_up, down_far = scatter_one(down_keep, down_came)
    grads[2], grads[1], keep, send = bottom_levels(
        where, grads[3], incoming, w_self, w_cross, w_up
    )
    came = _send(send, "tp", CORE)
    own, down, up, far = scatter_one(keep, came)
    below, above, far = scatter_y(down, up, far)
    grads[1], grads[2] = after((grads[1], grads[2]), own)
    upper_came = _send(upper_send, "seq", _xor(1))
    lower_keep, lower_send = outer_terms(
        me, [[s0], [s1], [s2]], [1, 2, [partner2]], [[grads[1]], [grads[2]], grads[3]], parts,
    )
    lower_came = _send(lower_send, "seq", _xor(1))
    far = after(far, lower_send, upper_came)
    side = _send(scatter_two(own, below, above, far), "tp", XHI)
    side = after(side, down_own)
    grad_hidden = add_up(cotangent, own, below, above, far, side)

    grad_rows = swap_seq(grad_hidden)
    down_below, down_above, down_far = scatter_y(
        *after((down_down, down_up, down_far), grad_hidden)
    )
    moved_back = mix(factor_t, after(grad_rows, lower_came))
    weights_keep, weights_send = halve_first(
        (lower_keep, upper_keep), (lower_came, upper_came)
    )
    weights_came = _send(weights_send, "seq", _xor(8))
    grad_first_out = swap_seq(moved_back)
    extra = second_terms(grad_rows, first_rows)
    ride = scatter_two(down_own, down_below, down_above, down_far)
    grad_first_out = after(grad_first_out, extra, ride, weights_came)
    side_block = carry_rows(grad_first_out, extra, ride)
    side = _send(side_block, "tp", XHI)
    weights_keep, weights_send = halve((weights_keep,), (weights_came,))
    weights_came = _send(weights_send, "seq", _xor(2))
    tall = 576
    pair = split_rows(side_block, side, tall)
    pair_y = gather_y(pair)
    weights_keep, weights_send = halve((weights_keep,), (weights_came,))
    weights_came = _send(weights_send, "seq", _xor(4))
    grad_mix = lax.dot_general(
        w_first[0], grad_first_out, (((0,), (0,)), ((), ())), preferred_element_type=F32
    )
    grad_tokens = (grad_hidden.astype(F32) + grad_mix).astype(BF)
    layer_out = add_up(
        hidden, down_own, down_below, down_above, down_far, side, start=tall
    )
    pair_y = after(pair_y, grad_tokens, layer_out, weights_came)
    first_keep, first_send = first_grad((pair, *pair_y), (early_pair, *early_y))
    first_came = _send(first_send, "tp", CORE)
    weights_keep = after(weights_keep, first_send)
    grad_self, grad_cross = last_half(weights_keep, weights_came, slots, token_scale)
    grad_first, small = finish_first(first_keep, first_came, width_scale)
    grad_second = small.reshape(16, 16, 32).transpose(2, 1, 0)
    return layer_out, grad_tokens, grad_first[None], grad_second, grad_self, grad_cross


def solution(mesh):
    in_specs = (
        P("seq", "tp"),
        P("seq", None, None),
        P("seq", None, None),
        P("tp", None, None, None),
        P(None, "tp", None, None),
        P(None, "tp", None, None),
        P("tp", None, None, None),
        P("tp", None),
        P("seq", "tp"),
    )
    out_specs = (
        P("seq", "tp"),
        P("seq", "tp"),
        P("seq", None, None),
        P("seq", None, None),
        P(None, "tp", "seq", None),
        P(None, "tp", "seq", None),
    )
    return jax.shard_map(
        layer, mesh=mesh, in_specs=in_specs, out_specs=out_specs, check_vma=False
    )
```

```python
import math

import jax
import jax.numpy as jnp
from jax import lax
from jax.experimental import pallas as pl
from jax.experimental.pallas import tpu as pltpu
from jax.sharding import PartitionSpec as P


BF = jnp.bfloat16
F32 = jnp.float32
MIB = 1 << 20
ROOT = math.sqrt(2.0 / math.pi)


def _send(value, axis, target):
    return lax.ppermute(value, axis, [(s, target(s)) for s in range(16)])


def _xor(mask):
    return lambda t: t ^ mask


def _ymove(step):
    return lambda t: (t & 9) | (((((t >> 1) & 3) + step) & 3) << 1)


CORE, XHI = _xor(1), _xor(8)


def after(value, *others):
    return lax.optimization_barrier((value, others))[0]


def position(block):
    me = lax.axis_index("tp")
    dx = ((block ^ me) >> 3) & 1
    dc = (block ^ me) & 1
    dy = ((block >> 1) - (me >> 1)) & 3
    key = dx * 4 + dy
    order = jnp.zeros_like(key)
    for k, at in enumerate((0, 4, 6, 2, 1, 5, 7, 3)):
        order = order + jnp.where(key == k, at, 0)
    return (order + 8 * dc).astype(jnp.int32)


def _shape(*shape, dtype=BF):
    return jax.ShapeDtypeStruct(shape, dtype)


VMEM = pl.BlockSpec(memory_space=pltpu.VMEM)
SMEM = pl.BlockSpec(memory_space=pltpu.SMEM)


def _call(body, outs, args, scalars=0, scratch=(), flops=0, limit=8):
    moved = sum(a.size * a.dtype.itemsize for a in args) + sum(
        math.prod(o.shape) * o.dtype.itemsize for o in outs
    )
    return pl.pallas_call(
        body,
        in_specs=[SMEM] * scalars + [VMEM] * (len(args) - scalars),
        out_specs=[VMEM] * len(outs),
        out_shape=list(outs),
        scratch_shapes=list(scratch),
        compiler_params=pltpu.CompilerParams(vmem_limit_bytes=limit * MIB),
        cost_estimate=pl.CostEstimate(
            flops=flops, bytes_accessed=moved, transcendentals=0
        ),
    )(*args)


def _dot(a, b):
    return lax.dot_general(a, b, (((1,), (0,)), ((), ())), preferred_element_type=F32)


def _dot_t(a, b):
    return lax.dot_general(a, b, (((1,), (1,)), ((), ())), preferred_element_type=F32)


def _dot_l(a, b):
    return lax.dot_general(a, b, (((0,), (0,)), ((), ())), preferred_element_type=F32)


def _cat(a, b):
    return jnp.concatenate([a, b], axis=1)


def _stack(a, b):
    return jnp.concatenate([a, b], axis=0)


def join(*pieces, start=0):
    total = sum(p.shape[0] for p in pieces)
    rows = pieces[0].shape[1] - start

    def body(*refs):
        at = 0
        for ref in refs[:-1]:
            for i in range(ref.shape[0]):
                refs[-1][at] = ref[i, start:, :]
                at += 1

    return _call(body, [_shape(total, rows, 128)], pieces)[0]


def gather_y(pair):
    below = _send(pair, "tp", _ymove(1))
    above = _send(pair, "tp", _ymove(3))
    far = _send(pair, "tp", _ymove(2))
    return below, above, far


def gather_core(*pieces, start=0):
    own = join(*pieces, start=start)
    return own, _send(own, "tp", CORE)


def _hold(refs, held, start, rows):
    at = 0
    for ref in refs:
        for i in range(ref.shape[0]):
            held[at] = ref[i, start : start + rows, :]
            at += 1


def up_levels(where, blocks, w_up, w_self, w_cross):
    slots, tokens = w_up.shape[0], blocks[0].shape[1]
    n = len(blocks)

    def body(where_ref, *refs):
        ins, (up, ws, wc, s0, s1, s2, held) = refs[:n], refs[n:]
        _hold(ins, held, 0, tokens)

        for j in range(slots):
            left, right = held[where_ref[2 * j]], held[where_ref[2 * j + 1]]
            s0[j] = _dot(_cat(left, right), _stack(up[j, 0], up[j, 1])).astype(BF)
        for level, (src, dst) in enumerate(((s0, s1), (s1, s2))):
            for j in range(slots):
                both = _cat(src[j], src[j ^ (1 << level)])
                dst[j] = _dot(both, _stack(ws[level, j], wc[level, j])).astype(BF)

    return _call(
        body,
        [_shape(slots, tokens, 128)] * 3,
        (where, *blocks, w_up, w_self, w_cross),
        scalars=1,
        scratch=[pltpu.VMEM((16, tokens, 128), BF)],
        flops=3 * slots * tokens * 2 * 256 * 128,
    )


def split_weights(w_self, w_cross):
    levels, slots = w_self.shape[:2]

    def body(ws, wc, *outs):
        for n, out in enumerate(outs):

            def step(j, carry, n=n, out=out):
                out[j, 0:128, :] = ws[n + 2, j]
                out[j, 128:256, :] = wc[n + 2, j]
                return carry

            lax.fori_loop(0, slots, step, 0)

    outs = [_shape(slots, 256, 128)] * (levels - 2)
    return [None, None, *_call(body, outs, (w_self, w_cross))]


def level_up(state, partner, weight, parts=1):
    slots, tokens, _ = state.shape
    rows = tokens // parts

    def body(s, p, w, *outs):
        for c, out in enumerate(outs):
            at = slice(c * rows, c * rows + rows)
            for j in range(slots):
                out[j] = _dot(_cat(s[j, at, :], p[j, at, :]), w[j]).astype(BF)

    return _call(
        body,
        [_shape(slots, rows, 128)] * parts,
        (state, partner, weight),
        flops=slots * tokens * 2 * 256 * 128,
    )


def gather_grad(where, blocks, w_down, parts):
    slots = w_down.shape[0]
    tokens = blocks[0].shape[1]
    rows = tokens // parts
    n = len(blocks)

    def body(where_ref, *refs):
        ins, down, outs, held = refs[:n], refs[n], refs[n + 1 : -1], refs[-1]
        _hold(ins, held, 0, tokens)

        def step(j, carry):
            left, right = held[where_ref[2 * j]], held[where_ref[2 * j + 1]]
            total = _dot_t(_cat(left, right), _cat(down[j, 0], down[j, 1]))
            for c, out in enumerate(outs):
                out[j] = total[c * rows : c * rows + rows]
            return carry

        lax.fori_loop(0, slots, step, 0)

    return _call(
        body,
        [_shape(slots, rows, 128, dtype=F32)] * parts,
        (where, *blocks, w_down),
        scalars=1,
        scratch=[pltpu.VMEM((16, tokens, 128), BF)],
        flops=slots * tokens * 4 * 128 * 128,
    )


def top_level(state, partner, weight, grad_act):
    slots, tokens, _ = state.shape

    def body(s, p, w, ga, act, grad, across):
        for j in range(slots):
            v = _dot(_cat(s[j], p[j]), w[j]).astype(BF).astype(F32)
            square = v * v
            t = jnp.tanh(ROOT * (v + 0.044715 * (v * square)))
            act[j] = (0.5 * v * (1.0 + t)).astype(BF)
            slope = 0.5 * (1.0 + t) + (0.5 * ROOT) * v * (1.0 - t * t) * (
                1.0 + (3 * 0.044715) * square
            )
            g = (ga[j] * slope).astype(BF)
            grad[j] = g
            across[j] = _dot_t(g, w[j, 128:256, :]).astype(BF)

    return _call(
        body,
        [_shape(*state.shape)] * 3,
        (state, partner, weight, grad_act),
        flops=slots * tokens * 3 * 2 * 128 * 128,
    )


def level_down(grad, incoming, weight, below):
    slots, tokens, _ = grad.shape

    def body(g, inc, w, wb, out, across):
        for j in range(slots):
            new = (_dot_t(g[j], w[j, 0:128, :]) + inc[j].astype(F32)).astype(BF)
            out[j] = new
            across[j] = _dot_t(new, wb[j, 128:256, :]).astype(BF)

    return _call(
        body,
        [_shape(*grad.shape)] * 2,
        (grad, incoming, weight, below),
        flops=slots * tokens * 2 * 2 * 128 * 128,
    )


def bottom_levels(where, grads, incoming, w_self, w_cross, w_up):
    parts = len(grads)
    slots, rows, _ = grads[0].shape
    tokens = rows * parts

    def body(where_ref, *refs):
        gs, incs = refs[:parts], refs[parts : 2 * parts]
        ws, wc, up, g2, g1, keep, send, g0, total = refs[2 * parts :]

        for c in range(parts):
            for j in range(slots):
                new = _dot_t(gs[c][j], ws[2, j]) + incs[c][j].astype(F32)
                g2[j, c * rows : c * rows + rows, :] = new.astype(BF)
        for level, (src, dst) in ((1, (g2, g1)), (0, (g1, g0))):
            for j in range(slots):
                other = j ^ (1 << level)
                both = _cat(src[j], src[other])
                weight = _cat(ws[level, j], wc[level, other])
                dst[j] = _dot_t(both, weight).astype(BF)
        total[...] = jnp.zeros_like(total)
        for j in range(slots):
            for k in range(2):
                at = where_ref[2 * j + k]
                total[at] = total[at] + _dot_t(g0[j], up[j, k])
        keep[...] = total[0:8].astype(BF)
        send[...] = total[8:16].astype(BF)

    return _call(
        body,
        [_shape(slots, tokens, 128)] * 2 + [_shape(8, tokens, 128)] * 2,
        (where, *grads, *incoming, w_self, w_cross, w_up),
        scalars=1,
        scratch=[
            pltpu.VMEM((slots, tokens, 128), BF),
            pltpu.VMEM((16, tokens, 128), F32),
        ],
        flops=slots * tokens * 7 * 2 * 128 * 128,
        limit=12,
    )


def _scatter(where_ref, piece, slots, total, keep, send):
    total[...] = jnp.zeros_like(total)

    def step(i, carry):
        at = where_ref[i]
        total[at] = total[at] + piece(i)
        return carry

    def finish(i, carry):
        keep[i] = total[i].astype(BF)
        send[i] = total[i + 8].astype(BF)
        return carry

    lax.fori_loop(0, 2 * slots, step, 0)
    lax.fori_loop(0, 8, finish, 0)


def down_pieces(where, acts, w_down):
    parts = len(acts)
    slots, rows, _ = acts[0].shape
    tokens = rows * parts

    def body(where_ref, *refs):
        ins, (down, keep, send, total) = refs[:parts], refs[parts:]

        def piece(i):
            whole = jnp.concatenate([r[i >> 1] for r in ins], axis=0)
            return _dot(whole, down[i >> 1, i & 1])

        _scatter(where_ref, piece, slots, total, keep, send)

    return _call(
        body,
        [_shape(8, tokens, 128)] * 2,
        (where, *acts, w_down),
        scalars=1,
        scratch=[pltpu.VMEM((16, tokens, 128), F32)],
        flops=slots * tokens * 2 * 2 * 128 * 128,
        limit=12,
    )


def scatter_one(keep, came):
    tokens = keep.shape[1]

    def body(k, g, own, down, up, far):
        for i in range(2):
            own[i] = k[i].astype(F32) + g[i].astype(F32)
            for n, out in enumerate((down, up, far)):
                at = 2 + 2 * n + i
                out[i] = (k[at].astype(F32) + g[at].astype(F32)).astype(BF)

    return _call(
        body,
        [_shape(2, tokens, 128, dtype=F32)] + [_shape(2, tokens, 128)] * 3,
        (keep, came),
    )


def scatter_y(down, up, far):
    below = _send(up, "tp", _ymove(1))
    above = _send(down, "tp", _ymove(3))
    beyond = _send(far, "tp", _ymove(2))
    return below, above, beyond


def scatter_two(own, below, above, far):
    def body(own, below, above, far, out):
        total = own[1] + below[1].astype(F32)
        out[0] = (total + above[1].astype(F32) + far[1].astype(F32)).astype(BF)

    return _call(body, [_shape(1, *own.shape[1:])], (own, below, above, far))[0]


def add_up(base, own, below, above, far, side, start=0):
    tokens = base.shape[0]

    def body(base, own, below, above, far, side, out):
        total = own[0] + below[0].astype(F32) + above[0].astype(F32)
        total = total + far[0].astype(F32)
        total = total + side[0, start : start + tokens, :].astype(F32)
        out[...] = (base[...].astype(F32) + total).astype(BF)

    return _call(
        body, [_shape(tokens, 128)], (base, own, below, above, far, side)
    )[0]


def outer_terms(me, lefts, rights, grads, parts, more=()):
    flat, plan = [], []

    def add(arrays):
        first = len(flat)
        flat.extend(arrays)
        return first, len(arrays)

    for left, right, grad in zip(lefts, rights, grads):
        plan.append(
            (
                add(left),
                right if isinstance(right, int) else add(right),
                add(grad),
            )
        )
    slots = lefts[0][0].shape[0]
    tokens = sum(a.shape[1] for a in lefts[0])
    rows = tokens // parts
    mats = len(plan) * 2 * slots
    total_mats = mats + (more[0].shape[1] if more else 0)
    n = len(flat)

    def body(me_ref, *refs):
        ins, (keep, send, held) = refs[:n], refs[-3:]
        for old, new in zip(refs[n:-3], (keep, send)):

            def copy(pos, carry, old=old, new=new):
                new[pos, mats:] = old[pos]
                return carry

            lax.fori_loop(0, 8, copy, 0)

        def read(entry, j, c):
            first, count = entry
            if count == parts:
                return ins[first + c][j]
            return ins[first][j, c * rows : c * rows + rows, :]

        def step(j, carry):
            for level, (left, right, grad) in enumerate(plan):
                total = None
                for c in range(parts):
                    if isinstance(right, int):
                        other = read(left, j ^ right, c)
                    else:
                        other = read(right, j, c)
                    both = _cat(read(left, j, c), other)
                    term = _dot_l(both, read(grad, j, c))
                    total = term if total is None else total + term
                held[...] = total
                for half in range(2):
                    mat = (level * 2 + half) * slots + j
                    for pos in range(16):
                        z0, xl, z1, z2 = pos >> 3, (pos >> 2) & 1, (pos >> 1) & 1, pos & 1
                        rel = xl * 8 + z2 * 4 + z1 * 2 + z0
                        row = half * 128 + (me_ref[0] ^ rel) * 8
                        value = held[pl.ds(pl.multiple_of(row, 8), 8), :]
                        if pos < 8:
                            keep[pos, mat] = value.astype(BF)
                        else:
                            send[pos - 8, mat] = value.astype(BF)
            return carry

        lax.fori_loop(0, slots, step, 0)

    return _call(
        body,
        [_shape(8, total_mats, 8, 128)] * 2,
        (me, *flat, *more),
        scalars=1,
        scratch=[pltpu.VMEM((256, 128), F32)],
        flops=len(plan) * slots * tokens * 2 * 256 * 128,
    )


def halve(keeps, cames):
    n = len(keeps)
    size = keeps[0].shape[0] // 2
    mats = [k.shape[1] for k in keeps]

    def body(*refs):
        new_keep, new_send = refs[2 * n :]
        at = 0
        for k, c, m in zip(refs[:n], refs[n : 2 * n], mats):
            new_keep[:, at : at + m] = k[:size].astype(F32) + c[:size].astype(F32)
            new_send[:, at : at + m] = (
                k[size:].astype(F32) + c[size:].astype(F32)
            ).astype(BF)
            at += m

    total = sum(mats)
    return _call(
        body,
        [_shape(size, total, 8, 128, dtype=F32), _shape(size, total, 8, 128)],
        (*keeps, *cames),
    )


HBM = pl.BlockSpec(memory_space=pltpu.HBM)


def halve_first(keeps, cames):
    n = len(keeps)
    size = keeps[0].shape[0] // 2
    mats = [k.shape[1] for k in keeps]
    args = (*keeps, *cames)

    def body(*refs):
        ins, (new_keep, new_send), held = refs[: 2 * n], refs[2 * n : 2 * n + 2], refs[2 * n + 2 : -1]
        copies = [
            pltpu.make_async_copy(ref, buf, refs[-1].at[i])
            for i, (ref, buf) in enumerate(zip(ins, held))
        ]
        for copy in copies:
            copy.start()
        for copy in copies:
            copy.wait()
        at = 0
        for k, c, m in zip(held[:n], held[n:], mats):
            new_keep[:, at : at + m] = k[:size].astype(F32) + c[:size].astype(F32)
            new_send[:, at : at + m] = (
                k[size:].astype(F32) + c[size:].astype(F32)
            ).astype(BF)
            at += m

    total = sum(mats)
    return pl.pallas_call(
        body,
        in_specs=[HBM] * len(args),
        out_specs=[VMEM] * 2,
        out_shape=[
            _shape(size, total, 8, 128, dtype=F32),
            _shape(size, total, 8, 128),
        ],
        scratch_shapes=[pltpu.VMEM(a.shape, a.dtype) for a in args]
        + [pltpu.SemaphoreType.DMA((len(args),))],
        compiler_params=pltpu.CompilerParams(vmem_limit_bytes=8 * MIB),
        cost_estimate=pl.CostEstimate(
            flops=0, bytes_accessed=4 * MIB, transcendentals=0
        ),
    )(*args)


def last_half(keep, came, slots, scale):
    levels = keep.shape[1] // (2 * slots)

    def body(k, c, own, cross):
        for level in range(levels):
            for half, out in enumerate((own, cross)):
                at = (level * 2 + half) * slots
                rows = slice(at, at + slots)
                out[level] = (k[0, rows] + c[0, rows].astype(F32)) * scale

    return _call(body, [_shape(levels, slots, 8, 128, dtype=F32)] * 2, (keep, came))


def _mask(shape):
    row = lax.broadcasted_iota(jnp.int32, shape, 0)
    col = lax.broadcasted_iota(jnp.int32, shape, 1)
    return ((row ^ col) & 31) == 0


def _pick(shape):
    row = lax.broadcasted_iota(jnp.int32, shape, 0)
    col = lax.broadcasted_iota(jnp.int32, shape, 1)
    return (col >> 5) == row


def mix(factor, rows):
    def body(f, r, out):
        n, groups = f.shape
        wide = _dot(f[...], _pick((groups, n)).astype(BF))
        wide = jnp.where(_mask((n, n)), wide, 0.0).astype(BF)
        out[...] = _dot(wide, r[...]).astype(BF)

    return _call(
        body, [_shape(*rows.shape)], (factor, rows), flops=2 * 512 * 512 * 128
    )[0]


def second_terms(grads, rows):
    def body(g, r, out):
        n = r.shape[0]
        pick = _pick((16, n)).astype(BF)

        def step(k, carry):
            both = _dot_t(r[...], g[pl.ds(pl.multiple_of(k * 128, 128), 128), :])
            both = jnp.where(_mask((n, 128)), both, 0.0)
            high = both.astype(BF)
            low = (both - high.astype(F32)).astype(BF)
            small = _dot(pick, high) + _dot(pick, low)
            out[pl.ds(pl.multiple_of(k * 16, 16), 16), :] = small.astype(BF)
            return carry

        lax.fori_loop(0, 4, step, 0)

    return _call(body, [_shape(64, 128)], (grads, rows), flops=2 * 512 * 512 * 128)[0]


def first_grad(grads, tokens):
    n = len(grads)
    size = 512

    def body(*refs):
        gs, ts, (keep, send) = refs[:n], refs[n : 2 * n], refs[2 * n :]
        wide = lambda refs: jnp.concatenate(
            [r[i, 0:size, :] for r in refs for i in range(2)], axis=1
        )
        term = _dot_t(wide(gs), wide(ts))
        keep[0:size] = term
        send[0:size] = term.astype(BF)
        extra = None
        for g in gs:
            more = g[0, size:, :].astype(F32) + g[1, size:, :].astype(F32)
            extra = more if extra is None else extra + more
        for k in range(4):
            lanes = slice(k * 128, k * 128 + 128)
            keep[size:, lanes] = extra[k * 16 : k * 16 + 16]
            send[size:, lanes] = extra[k * 16 : k * 16 + 16].astype(BF)

    return _call(
        body,
        [_shape(size + 16, size, dtype=F32), _shape(size + 16, size)],
        (*grads, *tokens),
        flops=2 * size * size * 1024,
    )


def finish_first(keep, came, scale):
    size = keep.shape[1]

    def body(k, c, out, small):
        out[...] = (k[0:size] + c[0:size].astype(F32)) * scale
        small[...] = (k[size:] + c[size:].astype(F32)) * scale

    return _call(
        body,
        [_shape(size, size, dtype=F32), _shape(16, size, dtype=F32)],
        (keep, came),
    )


def carry_rows(grad, extra, ride):
    tall = grad.shape[0] + extra.shape[0] + ride.shape[1]

    def body(g, e, r, out):
        n, m = g.shape[0], e.shape[0]
        out[0, 0:n, :] = g[...]
        out[0, n : n + m, :] = e[...]
        out[0, n + m :, :] = r[0]

    return _call(body, [_shape(1, tall, 128)], (grad, extra, ride))[0]


def split_rows(sent, side, rows):
    def body(s, x, pair):
        pair[0] = s[0, 0:rows, :]
        pair[1] = x[0, 0:rows, :]

    return _call(body, [_shape(2, rows, 128)], (sent, side))[0]


def layer(
    tokens, w_first, second_factor, w_up, w_self, w_cross, w_down, block_pairs, cotangent
):
    seq_len, width = tokens.shape
    levels, slots = w_self.shape[:2]
    token_scale = 1.0 / math.sqrt(seq_len * lax.axis_size("seq"))
    width_scale = 1.0 / math.sqrt(width * lax.axis_size("tp"))
    parts = 2
    chunks = range(parts)
    me = lax.axis_index("seq").astype(jnp.int32).reshape(1)
    where = position(block_pairs.reshape(-1))
    factor = second_factor.transpose(1, 0, 2).reshape(512, 16)
    factor_t = second_factor.transpose(2, 0, 1).reshape(512, 16)
    partner_of = [None, None] + [_xor(1 << b) for b in range(levels - 2)]
    top = levels - 1

    weights = split_weights(w_self, w_cross)

    def swap_seq(rows):
        moved = lax.all_to_all(
            rows.reshape(16, 32, 128), "seq", split_axis=0, concat_axis=0, tiled=True
        )
        return moved.reshape(512, 128)

    first_out = jnp.dot(w_first[0], tokens, preferred_element_type=F32).astype(BF)
    first_rows = swap_seq(first_out)
    early_block = jnp.concatenate([tokens, cotangent], 0)[None]
    early_block = after(early_block, first_out)
    early_side = _send(early_block, "tp", XHI)
    early_pair = join(early_block, early_side)
    early_y = gather_y(early_pair)
    mixed = mix(factor, after(first_rows, early_pair, me, where, factor_t))
    mixed = after(swap_seq(mixed), early_y)
    hidden = (tokens.astype(F32) + mixed.astype(F32)).astype(BF)

    block = hidden[None]
    side = _send(block, "tp", XHI)
    pair = join(block, side)
    pair_y = after(gather_y(pair), weights)
    blocks = gather_core(pair, *pair_y)
    early = gather_core(early_pair, *after(early_y, blocks), start=seq_len)
    s0, s1, s2 = up_levels(where, blocks, w_up, w_self, w_cross)
    partner2 = _send(s2, "tp", partner_of[2])
    states, partners, grads = {}, {}, {}
    states[3] = level_up(s2, partner2, weights[2], parts)
    grad_act = gather_grad(where, early, w_down, parts)
    for level in range(3, levels):
        partners[level] = [_send(s, "tp", partner_of[level]) for s in states[level]]
        if level < top:
            states[level + 1] = [
                level_up(s, p, weights[level])[0]
                for s, p in zip(states[level], partners[level])
            ]
    acts, incoming = [None] * parts, [None] * parts
    grads[levels] = [None] * parts
    for c in chunks:
        acts[c], grads[levels][c], across = top_level(
            states[top][c], partners[top][c], weights[top], grad_act[c]
        )
        incoming[c] = _send(across, "tp", partner_of[top])
    down_keep, down_send = down_pieces(where, acts, w_down)
    down_came = _send(down_send, "tp", CORE)
    for level in range(top, 2, -1):
        grads[level] = [None] * parts
        if level == 4:
            incoming[0] = after(incoming[0], down_send)
        if level == 3:
            upper = [3, 4, 5]
            upper_keep, upper_send = outer_terms(
                me,
                [states[l] for l in upper],
                [partners[l] for l in upper],
                [grads[l + 1] for l in upper],
                parts,
            )
            incoming[1] = after(incoming[1], upper_send)
        for c in chunks:
            grads[level][c], across = level_down(
                grads[level + 1][c], incoming[c], weights[level], weights[level - 1]
            )
            incoming[c] = _send(across, "tp", partner_of[level - 1])
    down_own, down_down, down_up, down_far = scatter_one(down_keep, down_came)
    grads[2], grads[1], keep, send = bottom_levels(
        where, grads[3], incoming, w_self, w_cross, w_up
    )
    came = _send(send, "tp", CORE)
    own, down, up, far = scatter_one(keep, came)
    below, above, far = scatter_y(down, up, far)
    grads[1], grads[2] = after((grads[1], grads[2]), own)
    upper_came = _send(upper_send, "seq", _xor(1))
    lower_keep, lower_send = outer_terms(
        me, [[s0], [s1], [s2]], [1, 2, [partner2]], [[grads[1]], [grads[2]], grads[3]], parts,
    )
    lower_came = _send(lower_send, "seq", _xor(1))
    upper_keep, upper_send = halve((upper_keep,), (upper_came,))
    upper_came = _send(upper_send, "seq", _xor(8))
    far = after(far, lower_send, upper_send)
    to_side = scatter_two(own, below, above, far)
    side = _send(to_side, "tp", XHI)
    lower_keep, lower_send = halve((lower_keep,), (lower_came,))
    lower_came = _send(lower_send, "seq", _xor(8))
    side = after(side, down_own, lower_send)
    grad_hidden = add_up(cotangent, own, below, above, far, side)

    grad_rows = swap_seq(grad_hidden)
    down_below, down_above, down_far = scatter_y(
        *after((down_down, down_up, down_far), grad_hidden)
    )
    weights_keep, weights_send = halve_first(
        (lower_keep, upper_keep), (lower_came, upper_came)
    )
    weights_came = _send(weights_send, "seq", _xor(2))
    moved_back = mix(factor_t, after(grad_rows, weights_send))
    grad_first_out = swap_seq(moved_back)
    extra = second_terms(grad_rows, first_rows)
    ride = scatter_two(down_own, down_below, down_above, down_far)
    weights_keep, weights_send = halve((weights_keep,), (weights_came,))
    weights_came = _send(weights_send, "seq", _xor(4))
    grad_first_out = after(grad_first_out, extra, ride, weights_send)
    side_block = carry_rows(grad_first_out, extra, ride)
    side = _send(side_block, "tp", XHI)
    tall = 576
    pair = split_rows(side_block, side, tall)
    pair_y = gather_y(pair)
    grad_mix = lax.dot_general(
        w_first[0], grad_first_out, (((0,), (0,)), ((), ())), preferred_element_type=F32
    )
    grad_tokens = (grad_hidden.astype(F32) + grad_mix).astype(BF)
    layer_out = add_up(
        hidden, down_own, down_below, down_above, down_far, side, start=tall
    )
    pair_y = after(pair_y, grad_tokens, layer_out, weights_came)
    first_keep, first_send = first_grad((pair, *pair_y), (early_pair, *early_y))
    first_came = _send(first_send, "tp", CORE)
    weights_keep = after(weights_keep, first_send)
    grad_self, grad_cross = last_half(weights_keep, weights_came, slots, token_scale)
    grad_first, small = finish_first(first_keep, first_came, width_scale)
    grad_second = small.reshape(16, 16, 32).transpose(2, 1, 0)
    return layer_out, grad_tokens, grad_first[None], grad_second, grad_self, grad_cross


def solution(mesh):
    in_specs = (
        P("seq", "tp"),
        P("seq", None, None),
        P("seq", None, None),
        P("tp", None, None, None),
        P(None, "tp", None, None),
        P(None, "tp", None, None),
        P("tp", None, None, None),
        P("tp", None),
        P("seq", "tp"),
    )
    out_specs = (
        P("seq", "tp"),
        P("seq", "tp"),
        P("seq", None, None),
        P("seq", None, None),
        P(None, "tp", "seq", None),
        P(None, "tp", "seq", None),
    )
    return jax.shard_map(
        layer, mesh=mesh, in_specs=in_specs, out_specs=out_specs, check_vma=False
    )
```

```python
import math

import jax
import jax.numpy as jnp
from jax import lax
from jax.experimental import pallas as pl
from jax.experimental.pallas import tpu as pltpu
from jax.sharding import PartitionSpec as P


BF = jnp.bfloat16
F32 = jnp.float32
MIB = 1 << 20
ROOT = math.sqrt(2.0 / math.pi)


def _send(value, axis, target):
    return lax.ppermute(value, axis, [(s, target(s)) for s in range(16)])


def _xor(mask):
    return lambda t: t ^ mask


def _ymove(step):
    return lambda t: (t & 9) | (((((t >> 1) & 3) + step) & 3) << 1)


CORE, XHI = _xor(1), _xor(8)


def after(value, *others):
    return lax.optimization_barrier((value, others))[0]


def position(block):
    me = lax.axis_index("tp")
    dx = ((block ^ me) >> 3) & 1
    dc = (block ^ me) & 1
    dy = ((block >> 1) - (me >> 1)) & 3
    key = dx * 4 + dy
    order = jnp.zeros_like(key)
    for k, at in enumerate((0, 4, 6, 2, 1, 5, 7, 3)):
        order = order + jnp.where(key == k, at, 0)
    return (order + 8 * dc).astype(jnp.int32)


def _shape(*shape, dtype=BF):
    return jax.ShapeDtypeStruct(shape, dtype)


VMEM = pl.BlockSpec(memory_space=pltpu.VMEM)
SMEM = pl.BlockSpec(memory_space=pltpu.SMEM)


def _call(body, outs, args, scalars=0, scratch=(), flops=0, limit=8):
    moved = sum(a.size * a.dtype.itemsize for a in args) + sum(
        math.prod(o.shape) * o.dtype.itemsize for o in outs
    )
    return pl.pallas_call(
        body,
        in_specs=[SMEM] * scalars + [VMEM] * (len(args) - scalars),
        out_specs=[VMEM] * len(outs),
        out_shape=list(outs),
        scratch_shapes=list(scratch),
        compiler_params=pltpu.CompilerParams(vmem_limit_bytes=limit * MIB),
        cost_estimate=pl.CostEstimate(
            flops=flops, bytes_accessed=moved, transcendentals=0
        ),
    )(*args)


def _dot(a, b):
    return lax.dot_general(a, b, (((1,), (0,)), ((), ())), preferred_element_type=F32)


def _dot_t(a, b):
    return lax.dot_general(a, b, (((1,), (1,)), ((), ())), preferred_element_type=F32)


def _dot_l(a, b):
    return lax.dot_general(a, b, (((0,), (0,)), ((), ())), preferred_element_type=F32)


def _cat(a, b):
    return jnp.concatenate([a, b], axis=1)


def _stack(a, b):
    return jnp.concatenate([a, b], axis=0)


def join(*pieces, start=0):
    total = sum(p.shape[0] for p in pieces)
    rows = pieces[0].shape[1] - start

    def body(*refs):
        at = 0
        for ref in refs[:-1]:
            for i in range(ref.shape[0]):
                refs[-1][at] = ref[i, start:, :]
                at += 1

    return _call(body, [_shape(total, rows, 128)], pieces)[0]


def gather_y(pair):
    below = _send(pair, "tp", _ymove(1))
    above = _send(pair, "tp", _ymove(3))
    far = _send(pair, "tp", _ymove(2))
    return below, above, far


def gather_core(*pieces, start=0):
    own = join(*pieces, start=start)
    return own, _send(own, "tp", CORE)


def _hold(refs, held, start, rows):
    at = 0
    for ref in refs:
        for i in range(ref.shape[0]):
            held[at] = ref[i, start : start + rows, :]
            at += 1


def up_levels(where, blocks, w_up, w_self, w_cross):
    slots, tokens = w_up.shape[0], blocks[0].shape[1]
    n = len(blocks)

    def body(where_ref, *refs):
        ins, (up, ws, wc, s0, s1, s2, held) = refs[:n], refs[n:]
        _hold(ins, held, 0, tokens)

        for j in range(slots):
            left, right = held[where_ref[2 * j]], held[where_ref[2 * j + 1]]
            s0[j] = _dot(_cat(left, right), _stack(up[j, 0], up[j, 1])).astype(BF)
        for level, (src, dst) in enumerate(((s0, s1), (s1, s2))):
            for j in range(slots):
                both = _cat(src[j], src[j ^ (1 << level)])
                dst[j] = _dot(both, _stack(ws[level, j], wc[level, j])).astype(BF)

    return _call(
        body,
        [_shape(slots, tokens, 128)] * 3,
        (where, *blocks, w_up, w_self, w_cross),
        scalars=1,
        scratch=[pltpu.VMEM((16, tokens, 128), BF)],
        flops=3 * slots * tokens * 2 * 256 * 128,
    )


def split_weights(w_self, w_cross):
    levels, slots = w_self.shape[:2]

    def body(ws, wc, *outs):
        for n, out in enumerate(outs):

            def step(j, carry, n=n, out=out):
                out[j, 0:128, :] = ws[n + 2, j]
                out[j, 128:256, :] = wc[n + 2, j]
                return carry

            lax.fori_loop(0, slots, step, 0)

    outs = [_shape(slots, 256, 128)] * (levels - 2)
    return [None, None, *_call(body, outs, (w_self, w_cross))]


def level_up(state, partner, weight, parts=1):
    slots, tokens, _ = state.shape
    rows = tokens // parts

    def body(s, p, w, *outs):
        for c, out in enumerate(outs):
            at = slice(c * rows, c * rows + rows)
            for j in range(slots):
                out[j] = _dot(_cat(s[j, at, :], p[j, at, :]), w[j]).astype(BF)

    return _call(
        body,
        [_shape(slots, rows, 128)] * parts,
        (state, partner, weight),
        flops=slots * tokens * 2 * 256 * 128,
    )


def gather_grad(where, blocks, w_down, parts):
    slots = w_down.shape[0]
    tokens = blocks[0].shape[1]
    rows = tokens // parts
    n = len(blocks)

    def body(where_ref, *refs):
        ins, down, outs, held = refs[:n], refs[n], refs[n + 1 : -1], refs[-1]
        _hold(ins, held, 0, tokens)

        def step(j, carry):
            left, right = held[where_ref[2 * j]], held[where_ref[2 * j + 1]]
            total = _dot_t(_cat(left, right), _cat(down[j, 0], down[j, 1]))
            for c, out in enumerate(outs):
                out[j] = total[c * rows : c * rows + rows]
            return carry

        lax.fori_loop(0, slots, step, 0)

    return _call(
        body,
        [_shape(slots, rows, 128, dtype=F32)] * parts,
        (where, *blocks, w_down),
        scalars=1,
        scratch=[pltpu.VMEM((16, tokens, 128), BF)],
        flops=slots * tokens * 4 * 128 * 128,
    )


def top_level(state, partner, weight, grad_act):
    slots, tokens, _ = state.shape

    def body(s, p, w, ga, act, grad, across):
        for j in range(slots):
            v = _dot(_cat(s[j], p[j]), w[j]).astype(BF).astype(F32)
            square = v * v
            t = jnp.tanh(ROOT * (v + 0.044715 * (v * square)))
            act[j] = (0.5 * v * (1.0 + t)).astype(BF)
            slope = 0.5 * (1.0 + t) + (0.5 * ROOT) * v * (1.0 - t * t) * (
                1.0 + (3 * 0.044715) * square
            )
            g = (ga[j] * slope).astype(BF)
            grad[j] = g
            across[j] = _dot_t(g, w[j, 128:256, :]).astype(BF)

    return _call(
        body,
        [_shape(*state.shape)] * 3,
        (state, partner, weight, grad_act),
        flops=slots * tokens * 3 * 2 * 128 * 128,
    )


def level_down(grad, incoming, weight, below):
    slots, tokens, _ = grad.shape

    def body(g, inc, w, wb, out, across):
        for j in range(slots):
            new = (_dot_t(g[j], w[j, 0:128, :]) + inc[j].astype(F32)).astype(BF)
            out[j] = new
            across[j] = _dot_t(new, wb[j, 128:256, :]).astype(BF)

    return _call(
        body,
        [_shape(*grad.shape)] * 2,
        (grad, incoming, weight, below),
        flops=slots * tokens * 2 * 2 * 128 * 128,
    )


def bottom_levels(where, grads, incoming, w_self, w_cross, w_up):
    parts = len(grads)
    slots, rows, _ = grads[0].shape
    tokens = rows * parts

    def body(where_ref, *refs):
        gs, incs = refs[:parts], refs[parts : 2 * parts]
        ws, wc, up, g2, g1, keep, send, g0, total = refs[2 * parts :]

        for c in range(parts):
            for j in range(slots):
                new = _dot_t(gs[c][j], ws[2, j]) + incs[c][j].astype(F32)
                g2[j, c * rows : c * rows + rows, :] = new.astype(BF)
        for level, (src, dst) in ((1, (g2, g1)), (0, (g1, g0))):
            for j in range(slots):
                other = j ^ (1 << level)
                both = _cat(src[j], src[other])
                weight = _cat(ws[level, j], wc[level, other])
                dst[j] = _dot_t(both, weight).astype(BF)
        total[...] = jnp.zeros_like(total)
        for j in range(slots):
            for k in range(2):
                at = where_ref[2 * j + k]
                total[at] = total[at] + _dot_t(g0[j], up[j, k])
        keep[...] = total[0:8].astype(BF)
        send[...] = total[8:16].astype(BF)

    return _call(
        body,
        [_shape(slots, tokens, 128)] * 2 + [_shape(8, tokens, 128)] * 2,
        (where, *grads, *incoming, w_self, w_cross, w_up),
        scalars=1,
        scratch=[
            pltpu.VMEM((slots, tokens, 128), BF),
            pltpu.VMEM((16, tokens, 128), F32),
        ],
        flops=slots * tokens * 7 * 2 * 128 * 128,
        limit=12,
    )


def _scatter(where_ref, piece, slots, total, keep, send):
    total[...] = jnp.zeros_like(total)

    def step(i, carry):
        at = where_ref[i]
        total[at] = total[at] + piece(i)
        return carry

    def finish(i, carry):
        keep[i] = total[i].astype(BF)
        send[i] = total[i + 8].astype(BF)
        return carry

    lax.fori_loop(0, 2 * slots, step, 0)
    lax.fori_loop(0, 8, finish, 0)


def down_pieces(where, acts, w_down):
    parts = len(acts)
    slots, rows, _ = acts[0].shape
    tokens = rows * parts

    def body(where_ref, *refs):
        ins, (down, keep, send, total) = refs[:parts], refs[parts:]

        def piece(i):
            whole = jnp.concatenate([r[i >> 1] for r in ins], axis=0)
            return _dot(whole, down[i >> 1, i & 1])

        _scatter(where_ref, piece, slots, total, keep, send)

    return _call(
        body,
        [_shape(8, tokens, 128)] * 2,
        (where, *acts, w_down),
        scalars=1,
        scratch=[pltpu.VMEM((16, tokens, 128), F32)],
        flops=slots * tokens * 2 * 2 * 128 * 128,
        limit=12,
    )


def scatter_one(keep, came):
    tokens = keep.shape[1]

    def body(k, g, own, down, up, far):
        for i in range(2):
            own[i] = k[i].astype(F32) + g[i].astype(F32)
            for n, out in enumerate((down, up, far)):
                at = 2 + 2 * n + i
                out[i] = (k[at].astype(F32) + g[at].astype(F32)).astype(BF)

    return _call(
        body,
        [_shape(2, tokens, 128, dtype=F32)] + [_shape(2, tokens, 128)] * 3,
        (keep, came),
    )


def scatter_y(down, up, far):
    below = _send(up, "tp", _ymove(1))
    above = _send(down, "tp", _ymove(3))
    beyond = _send(far, "tp", _ymove(2))
    return below, above, beyond


def scatter_two(own, below, above, far):
    def body(own, below, above, far, out):
        total = own[1] + below[1].astype(F32)
        out[0] = (total + above[1].astype(F32) + far[1].astype(F32)).astype(BF)

    return _call(body, [_shape(1, *own.shape[1:])], (own, below, above, far))[0]


def add_up(base, own, below, above, far, side):
    tokens = base.shape[0]

    def body(base, own, below, above, far, side, out):
        total = own[0] + below[0].astype(F32) + above[0].astype(F32)
        total = total + far[0].astype(F32)
        total = total + side[0].astype(F32)
        out[...] = (base[...].astype(F32) + total).astype(BF)

    return _call(
        body, [_shape(tokens, 128)], (base, own, below, above, far, side)
    )[0]


def outer_terms(me, lefts, rights, grads, parts, more=()):
    flat, plan = [], []

    def add(arrays):
        first = len(flat)
        flat.extend(arrays)
        return first, len(arrays)

    for left, right, grad in zip(lefts, rights, grads):
        plan.append(
            (
                add(left),
                right if isinstance(right, int) else add(right),
                add(grad),
            )
        )
    slots = lefts[0][0].shape[0]
    tokens = sum(a.shape[1] for a in lefts[0])
    rows = tokens // parts
    mats = len(plan) * 2 * slots
    total_mats = mats + (more[0].shape[1] if more else 0)
    n = len(flat)

    def body(me_ref, *refs):
        ins, (keep, send, held) = refs[:n], refs[-3:]
        for old, new in zip(refs[n:-3], (keep, send)):

            def copy(pos, carry, old=old, new=new):
                new[pos, mats:] = old[pos]
                return carry

            lax.fori_loop(0, 8, copy, 0)

        def read(entry, j, c):
            first, count = entry
            if count == parts:
                return ins[first + c][j]
            return ins[first][j, c * rows : c * rows + rows, :]

        def step(j, carry):
            for level, (left, right, grad) in enumerate(plan):
                total = None
                for c in range(parts):
                    if isinstance(right, int):
                        other = read(left, j ^ right, c)
                    else:
                        other = read(right, j, c)
                    both = _cat(read(left, j, c), other)
                    term = _dot_l(both, read(grad, j, c))
                    total = term if total is None else total + term
                held[...] = total
                for half in range(2):
                    mat = (level * 2 + half) * slots + j
                    for pos in range(16):
                        z0, xl, z1, z2 = pos >> 3, (pos >> 2) & 1, (pos >> 1) & 1, pos & 1
                        rel = xl * 8 + z2 * 4 + z1 * 2 + z0
                        row = half * 128 + (me_ref[0] ^ rel) * 8
                        value = held[pl.ds(pl.multiple_of(row, 8), 8), :]
                        if pos < 8:
                            keep[pos, mat] = value.astype(BF)
                        else:
                            send[pos - 8, mat] = value.astype(BF)
            return carry

        lax.fori_loop(0, slots, step, 0)

    return _call(
        body,
        [_shape(8, total_mats, 8, 128)] * 2,
        (me, *flat, *more),
        scalars=1,
        scratch=[pltpu.VMEM((256, 128), F32)],
        flops=len(plan) * slots * tokens * 2 * 256 * 128,
    )


def halve(keeps, cames):
    n = len(keeps)
    size = keeps[0].shape[0] // 2
    mats = [k.shape[1] for k in keeps]

    def body(*refs):
        new_keep, new_send = refs[2 * n :]
        at = 0
        for k, c, m in zip(refs[:n], refs[n : 2 * n], mats):
            new_keep[:, at : at + m] = k[:size].astype(F32) + c[:size].astype(F32)
            new_send[:, at : at + m] = (
                k[size:].astype(F32) + c[size:].astype(F32)
            ).astype(BF)
            at += m

    total = sum(mats)
    return _call(
        body,
        [_shape(size, total, 8, 128, dtype=F32), _shape(size, total, 8, 128)],
        (*keeps, *cames),
    )


HBM = pl.BlockSpec(memory_space=pltpu.HBM)


def halve_first(keeps, cames):
    n = len(keeps)
    size = keeps[0].shape[0] // 2
    mats = [k.shape[1] for k in keeps]
    args = (*keeps, *cames)

    def body(*refs):
        ins, (new_keep, new_send), held = refs[: 2 * n], refs[2 * n : 2 * n + 2], refs[2 * n + 2 : -1]
        copies = [
            pltpu.make_async_copy(ref, buf, refs[-1].at[i])
            for i, (ref, buf) in enumerate(zip(ins, held))
        ]
        for copy in copies:
            copy.start()
        for copy in copies:
            copy.wait()
        at = 0
        for k, c, m in zip(held[:n], held[n:], mats):
            new_keep[:, at : at + m] = k[:size].astype(F32) + c[:size].astype(F32)
            new_send[:, at : at + m] = (
                k[size:].astype(F32) + c[size:].astype(F32)
            ).astype(BF)
            at += m

    total = sum(mats)
    return pl.pallas_call(
        body,
        in_specs=[HBM] * len(args),
        out_specs=[VMEM] * 2,
        out_shape=[
            _shape(size, total, 8, 128, dtype=F32),
            _shape(size, total, 8, 128),
        ],
        scratch_shapes=[pltpu.VMEM(a.shape, a.dtype) for a in args]
        + [pltpu.SemaphoreType.DMA((len(args),))],
        compiler_params=pltpu.CompilerParams(vmem_limit_bytes=8 * MIB),
        cost_estimate=pl.CostEstimate(
            flops=0, bytes_accessed=4 * MIB, transcendentals=0
        ),
    )(*args)


def last_half(keep, came, slots, scale):
    levels = keep.shape[1] // (2 * slots)

    def body(k, c, own, cross):
        for level in range(levels):
            for half, out in enumerate((own, cross)):
                at = (level * 2 + half) * slots
                rows = slice(at, at + slots)
                out[level] = (k[0, rows] + c[0, rows].astype(F32)) * scale

    return _call(body, [_shape(levels, slots, 8, 128, dtype=F32)] * 2, (keep, came))


def _mask(shape):
    row = lax.broadcasted_iota(jnp.int32, shape, 0)
    col = lax.broadcasted_iota(jnp.int32, shape, 1)
    return ((row ^ col) & 31) == 0


def _pick(shape):
    row = lax.broadcasted_iota(jnp.int32, shape, 0)
    col = lax.broadcasted_iota(jnp.int32, shape, 1)
    return (col >> 5) == row


def mix(factor, rows):
    def body(f, r, out):
        n, groups = f.shape
        wide = _dot(f[...], _pick((groups, n)).astype(BF))
        wide = jnp.where(_mask((n, n)), wide, 0.0).astype(BF)
        out[...] = _dot(wide, r[...]).astype(BF)

    return _call(
        body, [_shape(*rows.shape)], (factor, rows), flops=2 * 512 * 512 * 128
    )[0]


def second_terms(grads, rows):
    def body(g, r, out):
        n = r.shape[0]
        pick = _pick((16, n)).astype(BF)

        def step(k, carry):
            both = _dot_t(r[...], g[pl.ds(pl.multiple_of(k * 128, 128), 128), :])
            both = jnp.where(_mask((n, 128)), both, 0.0)
            high = both.astype(BF)
            low = (both - high.astype(F32)).astype(BF)
            small = _dot(pick, high) + _dot(pick, low)
            out[pl.ds(pl.multiple_of(k * 16, 16), 16), :] = small.astype(BF)
            return carry

        lax.fori_loop(0, 4, step, 0)

    return _call(body, [_shape(64, 128)], (grads, rows), flops=2 * 512 * 512 * 128)[0]


def first_grad(grads, tokens):
    n = len(grads)
    size = 512

    def body(*refs):
        gs, ts, (keep, send) = refs[:n], refs[n : 2 * n], refs[2 * n :]
        wide = lambda refs: jnp.concatenate(
            [r[i, 0:size, :] for r in refs for i in range(2)], axis=1
        )
        term = _dot_t(wide(gs), wide(ts))
        keep[0:size] = term
        send[0:size] = term.astype(BF)
        extra = None
        for g in gs:
            more = g[0, size:, :].astype(F32) + g[1, size:, :].astype(F32)
            extra = more if extra is None else extra + more
        for k in range(4):
            lanes = slice(k * 128, k * 128 + 128)
            keep[size:, lanes] = extra[k * 16 : k * 16 + 16]
            send[size:, lanes] = extra[k * 16 : k * 16 + 16].astype(BF)

    return _call(
        body,
        [_shape(size + 16, size, dtype=F32), _shape(size + 16, size)],
        (*grads, *tokens),
        flops=2 * size * size * 1024,
    )


def finish_first(keep, came, scale):
    size = keep.shape[1]

    def body(k, c, out, small):
        out[...] = (k[0:size] + c[0:size].astype(F32)) * scale
        small[...] = (k[size:] + c[size:].astype(F32)) * scale

    return _call(
        body,
        [_shape(size, size, dtype=F32), _shape(16, size, dtype=F32)],
        (keep, came),
    )


def carry_rows(grad, extra):
    tall = grad.shape[0] + extra.shape[0]

    def body(g, e, out):
        n = g.shape[0]
        out[0, 0:n, :] = g[...]
        out[0, n:, :] = e[...]

    return _call(body, [_shape(1, tall, 128)], (grad, extra))[0]


def layer(
    tokens, w_first, second_factor, w_up, w_self, w_cross, w_down, block_pairs, cotangent
):
    seq_len, width = tokens.shape
    levels, slots = w_self.shape[:2]
    token_scale = 1.0 / math.sqrt(seq_len * lax.axis_size("seq"))
    width_scale = 1.0 / math.sqrt(width * lax.axis_size("tp"))
    parts = 2
    chunks = range(parts)
    me = lax.axis_index("seq").astype(jnp.int32).reshape(1)
    where = position(block_pairs.reshape(-1))
    factor = second_factor.transpose(1, 0, 2).reshape(512, 16)
    factor_t = second_factor.transpose(2, 0, 1).reshape(512, 16)
    partner_of = [None, None] + [_xor(1 << b) for b in range(levels - 2)]
    top = levels - 1

    weights = split_weights(w_self, w_cross)

    def swap_seq(rows):
        moved = lax.all_to_all(
            rows.reshape(16, 32, 128), "seq", split_axis=0, concat_axis=0, tiled=True
        )
        return moved.reshape(512, 128)

    first_out = jnp.dot(w_first[0], tokens, preferred_element_type=F32).astype(BF)
    first_rows = swap_seq(first_out)
    early_block = jnp.concatenate([tokens, cotangent], 0)[None]
    early_block = after(early_block, first_out)
    early_side = _send(early_block, "tp", XHI)
    early_pair = join(early_block, early_side)
    early_y = gather_y(early_pair)
    mixed = mix(factor, after(first_rows, early_pair, me, where, factor_t))
    mixed = after(swap_seq(mixed), early_y)
    hidden = (tokens.astype(F32) + mixed.astype(F32)).astype(BF)

    block = hidden[None]
    side = _send(block, "tp", XHI)
    pair = join(block, side)
    pair_y = after(gather_y(pair), weights)
    blocks = gather_core(pair, *pair_y)
    early = gather_core(early_pair, *after(early_y, blocks), start=seq_len)
    s0, s1, s2 = up_levels(where, blocks, w_up, w_self, w_cross)
    partner2 = _send(s2, "tp", partner_of[2])
    states, partners, grads = {}, {}, {}
    states[3] = level_up(s2, partner2, weights[2], parts)
    grad_act = gather_grad(where, early, w_down, parts)
    for level in range(3, levels):
        partners[level] = [_send(s, "tp", partner_of[level]) for s in states[level]]
        if level < top:
            states[level + 1] = [
                level_up(s, p, weights[level])[0]
                for s, p in zip(states[level], partners[level])
            ]
    acts, incoming = [None] * parts, [None] * parts
    grads[levels] = [None] * parts
    for c in chunks:
        acts[c], grads[levels][c], across = top_level(
            states[top][c], partners[top][c], weights[top], grad_act[c]
        )
        incoming[c] = _send(across, "tp", partner_of[top])
    down_keep, down_send = down_pieces(where, acts, w_down)
    down_came = _send(down_send, "tp", CORE)
    for level in range(top, 2, -1):
        grads[level] = [None] * parts
        if level == 4:
            incoming[0] = after(incoming[0], down_send)
        if level == 3:
            upper = [3, 4, 5]
            upper_keep, upper_send = outer_terms(
                me,
                [states[l] for l in upper],
                [partners[l] for l in upper],
                [grads[l + 1] for l in upper],
                parts,
            )
            incoming[1] = after(incoming[1], upper_send)
        for c in chunks:
            grads[level][c], across = level_down(
                grads[level + 1][c], incoming[c], weights[level], weights[level - 1]
            )
            incoming[c] = _send(across, "tp", partner_of[level - 1])
    down_own, down_down, down_up, down_far = scatter_one(down_keep, down_came)
    grads[2], grads[1], keep, send = bottom_levels(
        where, grads[3], incoming, w_self, w_cross, w_up
    )
    came = _send(send, "tp", CORE)
    own, down, up, far = scatter_one(keep, came)
    below, above, far = scatter_y(down, up, far)
    grads[1], grads[2] = after((grads[1], grads[2]), own)
    upper_came = _send(upper_send, "seq", _xor(1))
    lower_keep, lower_send = outer_terms(
        me, [[s0], [s1], [s2]], [1, 2, [partner2]], [[grads[1]], [grads[2]], grads[3]], parts,
    )
    lower_came = _send(lower_send, "seq", _xor(1))
    upper_keep, upper_send = halve((upper_keep,), (upper_came,))
    upper_came = _send(upper_send, "seq", _xor(8))
    far = after(far, lower_send, upper_send)
    to_side = scatter_two(own, below, above, far)
    side = _send(to_side, "tp", XHI)
    lower_keep, lower_send = halve((lower_keep,), (lower_came,))
    lower_came = _send(lower_send, "seq", _xor(8))
    side = after(side, down_own, lower_send)
    grad_hidden = add_up(cotangent, own, below, above, far, side)

    grad_rows = swap_seq(grad_hidden)
    down_below, down_above, down_far = scatter_y(
        *after((down_down, down_up, down_far), grad_hidden)
    )
    weights_keep, weights_send = halve_first(
        (lower_keep, upper_keep), (lower_came, upper_came)
    )
    weights_came = _send(weights_send, "seq", _xor(2))
    moved_back = mix(factor_t, after(grad_rows, weights_send))
    grad_first_out = swap_seq(moved_back)
    extra = second_terms(grad_rows, first_rows)
    down_side = scatter_two(down_own, down_below, down_above, down_far)
    down_side = _send(down_side, "tp", XHI)
    grad_first_out = after(grad_first_out, extra)
    block = carry_rows(grad_first_out, extra)
    side = _send(block, "tp", XHI)
    weights_keep, weights_send = halve((weights_keep,), (weights_came,))
    pair = join(block, side)
    pair_y = gather_y(pair)
    weights_came = _send(weights_send, "seq", _xor(4))
    grad_mix = lax.dot_general(
        w_first[0], grad_first_out, (((0,), (0,)), ((), ())), preferred_element_type=F32
    )
    grad_tokens = (grad_hidden.astype(F32) + grad_mix).astype(BF)
    layer_out = add_up(
        hidden, down_own, down_below, down_above, down_far, down_side
    )
    pair_y = after(pair_y, grad_tokens, layer_out, weights_came)
    first_keep, first_send = first_grad((pair, *pair_y), (early_pair, *early_y))
    first_came = _send(first_send, "tp", CORE)
    weights_keep = after(weights_keep, first_send)
    grad_self, grad_cross = last_half(weights_keep, weights_came, slots, token_scale)
    grad_first, small = finish_first(first_keep, first_came, width_scale)
    grad_second = small.reshape(16, 16, 32).transpose(2, 1, 0)
    return layer_out, grad_tokens, grad_first[None], grad_second, grad_self, grad_cross


def solution(mesh):
    in_specs = (
        P("seq", "tp"),
        P("seq", None, None),
        P("seq", None, None),
        P("tp", None, None, None),
        P(None, "tp", None, None),
        P(None, "tp", None, None),
        P("tp", None, None, None),
        P("tp", None),
        P("seq", "tp"),
    )
    out_specs = (
        P("seq", "tp"),
        P("seq", "tp"),
        P("seq", None, None),
        P("seq", None, None),
        P(None, "tp", "seq", None),
        P(None, "tp", "seq", None),
    )
    return jax.shard_map(
        layer, mesh=mesh, in_specs=in_specs, out_specs=out_specs, check_vma=False
    )
```

```python
import math

import jax
import jax.numpy as jnp
from jax import lax
from jax.experimental import pallas as pl
from jax.experimental.pallas import tpu as pltpu
from jax.sharding import PartitionSpec as P


BF = jnp.bfloat16
F32 = jnp.float32
MIB = 1 << 20
ROOT = math.sqrt(2.0 / math.pi)


def _send(value, axis, target):
    return lax.ppermute(value, axis, [(s, target(s)) for s in range(16)])


def _xor(mask):
    return lambda t: t ^ mask


def _ymove(step):
    return lambda t: (t & 9) | (((((t >> 1) & 3) + step) & 3) << 1)


CORE, XHI = _xor(1), _xor(8)


def after(value, *others):
    return lax.optimization_barrier((value, others))[0]


def position(block):
    me = lax.axis_index("tp")
    dx = ((block ^ me) >> 3) & 1
    dc = (block ^ me) & 1
    dy = ((block >> 1) - (me >> 1)) & 3
    key = dx * 4 + dy
    order = jnp.zeros_like(key)
    for k, at in enumerate((0, 4, 6, 2, 1, 5, 7, 3)):
        order = order + jnp.where(key == k, at, 0)
    return (order + 8 * dc).astype(jnp.int32)


def _shape(*shape, dtype=BF):
    return jax.ShapeDtypeStruct(shape, dtype)


VMEM = pl.BlockSpec(memory_space=pltpu.VMEM)
SMEM = pl.BlockSpec(memory_space=pltpu.SMEM)


def _call(body, outs, args, scalars=0, scratch=(), flops=0, limit=8):
    moved = sum(a.size * a.dtype.itemsize for a in args) + sum(
        math.prod(o.shape) * o.dtype.itemsize for o in outs
    )
    return pl.pallas_call(
        body,
        in_specs=[SMEM] * scalars + [VMEM] * (len(args) - scalars),
        out_specs=[VMEM] * len(outs),
        out_shape=list(outs),
        scratch_shapes=list(scratch),
        compiler_params=pltpu.CompilerParams(vmem_limit_bytes=limit * MIB),
        cost_estimate=pl.CostEstimate(
            flops=flops, bytes_accessed=moved, transcendentals=0
        ),
    )(*args)


def _dot(a, b):
    return lax.dot_general(a, b, (((1,), (0,)), ((), ())), preferred_element_type=F32)


def _dot_t(a, b):
    return lax.dot_general(a, b, (((1,), (1,)), ((), ())), preferred_element_type=F32)


def _dot_l(a, b):
    return lax.dot_general(a, b, (((0,), (0,)), ((), ())), preferred_element_type=F32)


def _cat(a, b):
    return jnp.concatenate([a, b], axis=1)


def _stack(a, b):
    return jnp.concatenate([a, b], axis=0)


def join(*pieces):
    total = sum(p.shape[0] for p in pieces)
    rows = pieces[0].shape[1]

    def body(*refs):
        at = 0
        for ref in refs[:-1]:
            for i in range(ref.shape[0]):
                refs[-1][at] = ref[i]
                at += 1

    return _call(body, [_shape(total, rows, 128)], pieces)[0]


def gather_y(pair):
    below = _send(pair, "tp", _ymove(1))
    above = _send(pair, "tp", _ymove(3))
    far = _send(pair, "tp", _ymove(2))
    return below, above, far


def split_pairs(block, side, rows):
    def body(b, s, last, first):
        for i, ref in enumerate((b, s)):
            first[i] = ref[0, 0:rows, :]
            last[i] = ref[0, rows:, :]

    return _call(body, [_shape(2, block.shape[1] - rows, 128), _shape(2, rows, 128)], (block, side))


def gather_core(*pieces):
    own = join(*pieces)
    return own, _send(own, "tp", CORE)


def _hold(refs, held, start, rows):
    at = 0
    for ref in refs:
        for i in range(ref.shape[0]):
            held[at] = ref[i, start : start + rows, :]
            at += 1


def up_levels(where, blocks, w_up, w_self, w_cross):
    slots, tokens = w_up.shape[0], blocks[0].shape[1]
    n = len(blocks)

    def body(where_ref, *refs):
        ins, (up, ws, wc, s0, s1, s2, held) = refs[:n], refs[n:]
        _hold(ins, held, 0, tokens)

        for j in range(slots):
            left, right = held[where_ref[2 * j]], held[where_ref[2 * j + 1]]
            s0[j] = _dot(_cat(left, right), _stack(up[j, 0], up[j, 1])).astype(BF)
        for level, (src, dst) in enumerate(((s0, s1), (s1, s2))):
            for j in range(slots):
                both = _cat(src[j], src[j ^ (1 << level)])
                dst[j] = _dot(both, _stack(ws[level, j], wc[level, j])).astype(BF)

    return _call(
        body,
        [_shape(slots, tokens, 128)] * 3,
        (where, *blocks, w_up, w_self, w_cross),
        scalars=1,
        scratch=[pltpu.VMEM((16, tokens, 128), BF)],
        flops=3 * slots * tokens * 2 * 256 * 128,
    )


def split_weights(w_self, w_cross):
    levels, slots = w_self.shape[:2]

    def body(ws, wc, *outs):
        for n, out in enumerate(outs):

            def step(j, carry, n=n, out=out):
                out[j, 0:128, :] = ws[n + 2, j]
                out[j, 128:256, :] = wc[n + 2, j]
                return carry

            lax.fori_loop(0, slots, step, 0)

    outs = [_shape(slots, 256, 128)] * (levels - 2)
    return [None, None, *_call(body, outs, (w_self, w_cross))]


def level_up(state, partner, weight, parts=1):
    slots, tokens, _ = state.shape
    rows = tokens // parts

    def body(s, p, w, *outs):
        for c, out in enumerate(outs):
            at = slice(c * rows, c * rows + rows)
            for j in range(slots):
                out[j] = _dot(_cat(s[j, at, :], p[j, at, :]), w[j]).astype(BF)

    return _call(
        body,
        [_shape(slots, rows, 128)] * parts,
        (state, partner, weight),
        flops=slots * tokens * 2 * 256 * 128,
    )


def gather_grad(where, blocks, w_down, parts):
    slots = w_down.shape[0]
    tokens = blocks[0].shape[1]
    rows = tokens // parts
    n = len(blocks)

    def body(where_ref, *refs):
        ins, down, outs, held = refs[:n], refs[n], refs[n + 1 : -1], refs[-1]
        _hold(ins, held, 0, tokens)

        def step(j, carry):
            left, right = held[where_ref[2 * j]], held[where_ref[2 * j + 1]]
            total = _dot_t(_cat(left, right), _cat(down[j, 0], down[j, 1]))
            for c, out in enumerate(outs):
                out[j] = total[c * rows : c * rows + rows]
            return carry

        lax.fori_loop(0, slots, step, 0)

    return _call(
        body,
        [_shape(slots, rows, 128, dtype=F32)] * parts,
        (where, *blocks, w_down),
        scalars=1,
        scratch=[pltpu.VMEM((16, tokens, 128), BF)],
        flops=slots * tokens * 4 * 128 * 128,
    )


def top_level(state, partner, weight, grad_act):
    slots, tokens, _ = state.shape

    def body(s, p, w, ga, act, grad, across):
        for j in range(slots):
            v = _dot(_cat(s[j], p[j]), w[j]).astype(BF).astype(F32)
            square = v * v
            t = jnp.tanh(ROOT * (v + 0.044715 * (v * square)))
            act[j] = (0.5 * v * (1.0 + t)).astype(BF)
            slope = 0.5 * (1.0 + t) + (0.5 * ROOT) * v * (1.0 - t * t) * (
                1.0 + (3 * 0.044715) * square
            )
            g = (ga[j] * slope).astype(BF)
            grad[j] = g
            across[j] = _dot_t(g, w[j, 128:256, :]).astype(BF)

    return _call(
        body,
        [_shape(*state.shape)] * 3,
        (state, partner, weight, grad_act),
        flops=slots * tokens * 3 * 2 * 128 * 128,
    )


def level_down(grad, incoming, weight, below):
    slots, tokens, _ = grad.shape

    def body(g, inc, w, wb, out, across):
        for j in range(slots):
            new = (_dot_t(g[j], w[j, 0:128, :]) + inc[j].astype(F32)).astype(BF)
            out[j] = new
            across[j] = _dot_t(new, wb[j, 128:256, :]).astype(BF)

    return _call(
        body,
        [_shape(*grad.shape)] * 2,
        (grad, incoming, weight, below),
        flops=slots * tokens * 2 * 2 * 128 * 128,
    )


def bottom_levels(where, grads, incoming, w_self, w_cross, w_up):
    parts = len(grads)
    slots, rows, _ = grads[0].shape
    tokens = rows * parts

    def body(where_ref, *refs):
        gs, incs = refs[:parts], refs[parts : 2 * parts]
        ws, wc, up, g2, g1, keep, send, g0, total = refs[2 * parts :]

        for c in range(parts):
            for j in range(slots):
                new = _dot_t(gs[c][j], ws[2, j]) + incs[c][j].astype(F32)
                g2[j, c * rows : c * rows + rows, :] = new.astype(BF)
        for level, (src, dst) in ((1, (g2, g1)), (0, (g1, g0))):
            for j in range(slots):
                other = j ^ (1 << level)
                both = _cat(src[j], src[other])
                weight = _cat(ws[level, j], wc[level, other])
                dst[j] = _dot_t(both, weight).astype(BF)
        total[...] = jnp.zeros_like(total)
        for j in range(slots):
            for k in range(2):
                at = where_ref[2 * j + k]
                total[at] = total[at] + _dot_t(g0[j], up[j, k])
        keep[...] = total[0:8].astype(BF)
        send[...] = total[8:16].astype(BF)

    return _call(
        body,
        [_shape(slots, tokens, 128)] * 2 + [_shape(8, tokens, 128)] * 2,
        (where, *grads, *incoming, w_self, w_cross, w_up),
        scalars=1,
        scratch=[
            pltpu.VMEM((slots, tokens, 128), BF),
            pltpu.VMEM((16, tokens, 128), F32),
        ],
        flops=slots * tokens * 7 * 2 * 128 * 128,
        limit=12,
    )


def _scatter(where_ref, piece, slots, total, keep, send):
    total[...] = jnp.zeros_like(total)

    def step(i, carry):
        at = where_ref[i]
        total[at] = total[at] + piece(i)
        return carry

    def finish(i, carry):
        keep[i] = total[i].astype(BF)
        send[i] = total[i + 8].astype(BF)
        return carry

    lax.fori_loop(0, 2 * slots, step, 0)
    lax.fori_loop(0, 8, finish, 0)


def down_pieces(where, acts, w_down):
    parts = len(acts)
    slots, rows, _ = acts[0].shape
    tokens = rows * parts

    def body(where_ref, *refs):
        ins, (down, keep, send, total) = refs[:parts], refs[parts:]

        def piece(i):
            whole = jnp.concatenate([r[i >> 1] for r in ins], axis=0)
            return _dot(whole, down[i >> 1, i & 1])

        _scatter(where_ref, piece, slots, total, keep, send)

    return _call(
        body,
        [_shape(8, tokens, 128)] * 2,
        (where, *acts, w_down),
        scalars=1,
        scratch=[pltpu.VMEM((16, tokens, 128), F32)],
        flops=slots * tokens * 2 * 2 * 128 * 128,
        limit=12,
    )


def scatter_one(keep, came, rider=None):
    tokens = keep.shape[1]
    riders = () if rider is None else (rider,)
    tall = 2 + sum(r.shape[0] for r in riders)

    def body(k, g, *refs):
        own, down, up, far = refs[-4:]
        for ride in refs[:-4]:
            for out in (down, up, far):
                out[2:] = ride[...]
        for i in range(2):
            own[i] = k[i].astype(F32) + g[i].astype(F32)
            for n, out in enumerate((down, up, far)):
                at = 2 + 2 * n + i
                out[i] = (k[at].astype(F32) + g[at].astype(F32)).astype(BF)

    return _call(
        body,
        [_shape(2, tokens, 128, dtype=F32)] + [_shape(tall, tokens, 128)] * 3,
        (keep, came, *riders),
    )


def scatter_y(down, up, far):
    below = _send(up, "tp", _ymove(1))
    above = _send(down, "tp", _ymove(3))
    beyond = _send(far, "tp", _ymove(2))
    return below, above, beyond


def scatter_two(own, below, above, far):
    def body(own, below, above, far, out):
        total = own[1] + below[1].astype(F32)
        out[0] = (total + above[1].astype(F32) + far[1].astype(F32)).astype(BF)

    return _call(body, [_shape(1, *own.shape[1:])], (own, below, above, far))[0]


def add_up(base, own, below, above, far, side):
    tokens = base.shape[0]

    def body(base, own, below, above, far, side, out):
        total = own[0] + below[0].astype(F32) + above[0].astype(F32)
        total = total + far[0].astype(F32)
        total = total + side[0].astype(F32)
        out[...] = (base[...].astype(F32) + total).astype(BF)

    return _call(
        body, [_shape(tokens, 128)], (base, own, below, above, far, side)
    )[0]


def outer_terms(me, lefts, rights, grads, parts, more=()):
    flat, plan = [], []

    def add(arrays):
        first = len(flat)
        flat.extend(arrays)
        return first, len(arrays)

    for left, right, grad in zip(lefts, rights, grads):
        plan.append(
            (
                add(left),
                right if isinstance(right, int) else add(right),
                add(grad),
            )
        )
    slots = lefts[0][0].shape[0]
    tokens = sum(a.shape[1] for a in lefts[0])
    rows = tokens // parts
    mats = len(plan) * 2 * slots
    total_mats = mats + (more[0].shape[1] if more else 0)
    n = len(flat)

    def body(me_ref, *refs):
        ins, (keep, send, held) = refs[:n], refs[-3:]
        for old, new in zip(refs[n:-3], (keep, send)):

            def copy(pos, carry, old=old, new=new):
                new[pos, mats:] = old[pos]
                return carry

            lax.fori_loop(0, 8, copy, 0)

        def read(entry, j, c):
            first, count = entry
            if count == parts:
                return ins[first + c][j]
            return ins[first][j, c * rows : c * rows + rows, :]

        def step(j, carry):
            for level, (left, right, grad) in enumerate(plan):
                total = None
                for c in range(parts):
                    if isinstance(right, int):
                        other = read(left, j ^ right, c)
                    else:
                        other = read(right, j, c)
                    both = _cat(read(left, j, c), other)
                    term = _dot_l(both, read(grad, j, c))
                    total = term if total is None else total + term
                held[...] = total
                for half in range(2):
                    mat = (level * 2 + half) * slots + j
                    for pos in range(16):
                        z0, xl, z1, z2 = pos >> 3, (pos >> 2) & 1, (pos >> 1) & 1, pos & 1
                        rel = xl * 8 + z2 * 4 + z1 * 2 + z0
                        row = half * 128 + (me_ref[0] ^ rel) * 8
                        value = held[pl.ds(pl.multiple_of(row, 8), 8), :]
                        if pos < 8:
                            keep[pos, mat] = value.astype(BF)
                        else:
                            send[pos - 8, mat] = value.astype(BF)
            return carry

        lax.fori_loop(0, slots, step, 0)

    return _call(
        body,
        [_shape(8, total_mats, 8, 128)] * 2,
        (me, *flat, *more),
        scalars=1,
        scratch=[pltpu.VMEM((256, 128), F32)],
        flops=len(plan) * slots * tokens * 2 * 256 * 128,
    )


def halve(keeps, cames):
    n = len(keeps)
    size = keeps[0].shape[0] // 2
    mats = [k.shape[1] for k in keeps]

    def body(*refs):
        new_keep, new_send = refs[2 * n :]
        at = 0
        for k, c, m in zip(refs[:n], refs[n : 2 * n], mats):
            new_keep[:, at : at + m] = k[:size].astype(F32) + c[:size].astype(F32)
            new_send[:, at : at + m] = (
                k[size:].astype(F32) + c[size:].astype(F32)
            ).astype(BF)
            at += m

    total = sum(mats)
    return _call(
        body,
        [_shape(size, total, 8, 128, dtype=F32), _shape(size, total, 8, 128)],
        (*keeps, *cames),
    )


HBM = pl.BlockSpec(memory_space=pltpu.HBM)


def halve_first(keeps, cames):
    n = len(keeps)
    size = keeps[0].shape[0] // 2
    mats = [k.shape[1] for k in keeps]
    args = (*keeps, *cames)

    def body(*refs):
        ins, (new_keep, new_send), held = refs[: 2 * n], refs[2 * n : 2 * n + 2], refs[2 * n + 2 : -1]
        copies = [
            pltpu.make_async_copy(ref, buf, refs[-1].at[i])
            for i, (ref, buf) in enumerate(zip(ins, held))
        ]
        for copy in copies:
            copy.start()
        for copy in copies:
            copy.wait()
        at = 0
        for k, c, m in zip(held[:n], held[n:], mats):
            new_keep[:, at : at + m] = k[:size].astype(F32) + c[:size].astype(F32)
            new_send[:, at : at + m] = (
                k[size:].astype(F32) + c[size:].astype(F32)
            ).astype(BF)
            at += m

    total = sum(mats)
    return pl.pallas_call(
        body,
        in_specs=[HBM] * len(args),
        out_specs=[VMEM] * 2,
        out_shape=[
            _shape(size, total, 8, 128, dtype=F32),
            _shape(size, total, 8, 128),
        ],
        scratch_shapes=[pltpu.VMEM(a.shape, a.dtype) for a in args]
        + [pltpu.SemaphoreType.DMA((len(args),))],
        compiler_params=pltpu.CompilerParams(vmem_limit_bytes=8 * MIB),
        cost_estimate=pl.CostEstimate(
            flops=0, bytes_accessed=4 * MIB, transcendentals=0
        ),
    )(*args)


def last_half(keep, came, slots, scale):
    levels = keep.shape[1] // (2 * slots)

    def body(k, c, own, cross):
        for level in range(levels):
            for half, out in enumerate((own, cross)):
                at = (level * 2 + half) * slots
                rows = slice(at, at + slots)
                out[level] = (k[0, rows] + c[0, rows].astype(F32)) * scale

    return _call(body, [_shape(levels, slots, 8, 128, dtype=F32)] * 2, (keep, came))


def _mask(shape):
    row = lax.broadcasted_iota(jnp.int32, shape, 0)
    col = lax.broadcasted_iota(jnp.int32, shape, 1)
    return ((row ^ col) & 31) == 0


def _pick(shape):
    row = lax.broadcasted_iota(jnp.int32, shape, 0)
    col = lax.broadcasted_iota(jnp.int32, shape, 1)
    return (col >> 5) == row


def mix(factor, rows):
    def body(f, r, out):
        n, groups = f.shape
        wide = _dot(f[...], _pick((groups, n)).astype(BF))
        wide = jnp.where(_mask((n, n)), wide, 0.0).astype(BF)
        out[...] = _dot(wide, r[...]).astype(BF)

    return _call(
        body, [_shape(*rows.shape)], (factor, rows), flops=2 * 512 * 512 * 128
    )[0]


def second_terms(grads, rows):
    def body(g, r, out):
        n = r.shape[0]
        pick = _pick((16, n)).astype(BF)

        def step(k, carry):
            both = _dot_t(r[...], g[pl.ds(pl.multiple_of(k * 128, 128), 128), :])
            both = jnp.where(_mask((n, 128)), both, 0.0)
            high = both.astype(BF)
            low = (both - high.astype(F32)).astype(BF)
            small = _dot(pick, high) + _dot(pick, low)
            out[pl.ds(pl.multiple_of(k * 16, 16), 16), :] = small.astype(BF)
            return carry

        lax.fori_loop(0, 4, step, 0)

    return _call(body, [_shape(64, 128)], (grads, rows), flops=2 * 512 * 512 * 128)[0]


def first_grad(grads, tokens):
    n = len(grads)
    size = 512

    def body(*refs):
        gs, ts, (keep, send) = refs[:n], refs[n : 2 * n], refs[2 * n :]
        wide = lambda refs: jnp.concatenate(
            [r[r.shape[0] - 2 + i, 0:size, :] for r in refs for i in range(2)], axis=1
        )
        term = _dot_t(wide(gs), wide(ts))
        keep[0:size] = term
        send[0:size] = term.astype(BF)
        extra = None
        for g in gs:
            more = g[0, size:, :].astype(F32) + g[1, size:, :].astype(F32)
            extra = more if extra is None else extra + more
        for k in range(4):
            lanes = slice(k * 128, k * 128 + 128)
            keep[size:, lanes] = extra[k * 16 : k * 16 + 16]
            send[size:, lanes] = extra[k * 16 : k * 16 + 16].astype(BF)

    return _call(
        body,
        [_shape(size + 16, size, dtype=F32), _shape(size + 16, size)],
        (*grads, *tokens),
        flops=2 * size * size * 1024,
    )


def finish_first(keep, came, scale):
    size = keep.shape[1]

    def body(k, c, out, small):
        out[...] = (k[0:size] + c[0:size].astype(F32)) * scale
        small[...] = (k[size:] + c[size:].astype(F32)) * scale

    return _call(
        body,
        [_shape(size, size, dtype=F32), _shape(16, size, dtype=F32)],
        (keep, came),
    )


def carry_rows(grad, extra):
    tall = grad.shape[0] + extra.shape[0]

    def body(g, e, out):
        n = g.shape[0]
        out[0, 0:n, :] = g[...]
        out[0, n:, :] = e[...]

    return _call(body, [_shape(1, tall, 128)], (grad, extra))[0]


def layer(
    tokens, w_first, second_factor, w_up, w_self, w_cross, w_down, block_pairs, cotangent
):
    seq_len, width = tokens.shape
    levels, slots = w_self.shape[:2]
    token_scale = 1.0 / math.sqrt(seq_len * lax.axis_size("seq"))
    width_scale = 1.0 / math.sqrt(width * lax.axis_size("tp"))
    parts = 2
    chunks = range(parts)
    me = lax.axis_index("seq").astype(jnp.int32).reshape(1)
    where = position(block_pairs.reshape(-1))
    factor = second_factor.transpose(1, 0, 2).reshape(512, 16)
    factor_t = second_factor.transpose(2, 0, 1).reshape(512, 16)
    partner_of = [None, None] + [_xor(1 << b) for b in range(levels - 2)]
    top = levels - 1

    weights = split_weights(w_self, w_cross)

    def swap_seq(rows):
        moved = lax.all_to_all(
            rows.reshape(16, 32, 128), "seq", split_axis=0, concat_axis=0, tiled=True
        )
        return moved.reshape(512, 128)

    first_out = jnp.dot(w_first[0], tokens, preferred_element_type=F32).astype(BF)
    first_rows = swap_seq(first_out)
    early_block = jnp.concatenate([tokens, cotangent], 0)[None]
    early_block = after(early_block, first_out)
    early_side = _send(early_block, "tp", XHI)
    early_pair, token_pair = split_pairs(early_block, early_side, seq_len)
    early_y = gather_y(early_pair)
    mixed = mix(factor, after(first_rows, early_pair, me, where, factor_t))
    mixed = after(swap_seq(mixed), early_y)
    hidden = (tokens.astype(F32) + mixed.astype(F32)).astype(BF)

    block = hidden[None]
    side = _send(block, "tp", XHI)
    pair = join(block, side)
    pair_y = after(gather_y(pair), weights)
    blocks = gather_core(pair, *pair_y)
    early = gather_core(early_pair, *after(early_y, blocks))
    s0, s1, s2 = up_levels(where, blocks, w_up, w_self, w_cross)
    partner2 = _send(s2, "tp", partner_of[2])
    states, partners, grads = {}, {}, {}
    states[3] = level_up(s2, partner2, weights[2], parts)
    grad_act = gather_grad(where, early, w_down, parts)
    for level in range(3, levels):
        partners[level] = [_send(s, "tp", partner_of[level]) for s in states[level]]
        if level < top:
            states[level + 1] = [
                level_up(s, p, weights[level])[0]
                for s, p in zip(states[level], partners[level])
            ]
    acts, incoming = [None] * parts, [None] * parts
    grads[levels] = [None] * parts
    for c in chunks:
        acts[c], grads[levels][c], across = top_level(
            states[top][c], partners[top][c], weights[top], grad_act[c]
        )
        incoming[c] = _send(across, "tp", partner_of[top])
    down_keep, down_send = down_pieces(where, acts, w_down)
    down_came = _send(down_send, "tp", CORE)
    for level in range(top, 2, -1):
        grads[level] = [None] * parts
        if level == 4:
            incoming[0] = after(incoming[0], down_send)
        if level == 3:
            upper = [3, 4, 5]
            upper_keep, upper_send = outer_terms(
                me,
                [states[l] for l in upper],
                [partners[l] for l in upper],
                [grads[l + 1] for l in upper],
                parts,
            )
            incoming[1] = after(incoming[1], upper_send)
        for c in chunks:
            grads[level][c], across = level_down(
                grads[level + 1][c], incoming[c], weights[level], weights[level - 1]
            )
            incoming[c] = _send(across, "tp", partner_of[level - 1])
    down_own, down_down, down_up, down_far = scatter_one(
        down_keep, down_came, token_pair
    )
    grads[2], grads[1], keep, send = bottom_levels(
        where, grads[3], incoming, w_self, w_cross, w_up
    )
    came = _send(send, "tp", CORE)
    own, down, up, far = scatter_one(keep, came)
    below, above, far = scatter_y(down, up, far)
    grads[1], grads[2] = after((grads[1], grads[2]), own)
    upper_came = _send(upper_send, "seq", _xor(1))
    lower_keep, lower_send = outer_terms(
        me, [[s0], [s1], [s2]], [1, 2, [partner2]], [[grads[1]], [grads[2]], grads[3]], parts,
    )
    lower_came = _send(lower_send, "seq", _xor(1))
    upper_keep, upper_send = halve((upper_keep,), (upper_came,))
    upper_came = _send(upper_send, "seq", _xor(8))
    far = after(far, lower_send, upper_send)
    to_side = scatter_two(own, below, above, far)
    side = _send(to_side, "tp", XHI)
    lower_keep, lower_send = halve((lower_keep,), (lower_came,))
    lower_came = _send(lower_send, "seq", _xor(8))
    side = after(side, down_own, lower_send)
    grad_hidden = add_up(cotangent, own, below, above, far, side)

    grad_rows = swap_seq(grad_hidden)
    down_below, down_above, down_far = scatter_y(
        *after((down_down, down_up, down_far), grad_hidden)
    )
    weights_keep, weights_send = halve_first(
        (lower_keep, upper_keep), (lower_came, upper_came)
    )
    weights_came = _send(weights_send, "seq", _xor(2))
    moved_back = mix(factor_t, after(grad_rows, weights_send))
    grad_first_out = swap_seq(moved_back)
    extra = second_terms(grad_rows, first_rows)
    down_side = scatter_two(down_own, down_below, down_above, down_far)
    down_side = _send(down_side, "tp", XHI)
    grad_first_out = after(grad_first_out, extra)
    block = carry_rows(grad_first_out, extra)
    side = _send(block, "tp", XHI)
    weights_keep, weights_send = halve((weights_keep,), (weights_came,))
    pair = join(block, side)
    pair_y = gather_y(pair)
    weights_came = _send(weights_send, "seq", _xor(4))
    grad_mix = lax.dot_general(
        w_first[0], grad_first_out, (((0,), (0,)), ((), ())), preferred_element_type=F32
    )
    grad_tokens = (grad_hidden.astype(F32) + grad_mix).astype(BF)
    layer_out = add_up(
        hidden, down_own, down_below, down_above, down_far, down_side
    )
    pair_y = after(pair_y, grad_tokens, layer_out)
    first_keep, first_send = first_grad(
        (pair, *pair_y), (token_pair, down_below, down_above, down_far)
    )
    first_came = _send(first_send, "tp", CORE)
    weights_keep = after(weights_keep, first_send)
    grad_self, grad_cross = last_half(weights_keep, weights_came, slots, token_scale)
    grad_first, small = finish_first(first_keep, first_came, width_scale)
    grad_second = small.reshape(16, 16, 32).transpose(2, 1, 0)
    return layer_out, grad_tokens, grad_first[None], grad_second, grad_self, grad_cross


def solution(mesh):
    in_specs = (
        P("seq", "tp"),
        P("seq", None, None),
        P("seq", None, None),
        P("tp", None, None, None),
        P(None, "tp", None, None),
        P(None, "tp", None, None),
        P("tp", None, None, None),
        P("tp", None),
        P("seq", "tp"),
    )
    out_specs = (
        P("seq", "tp"),
        P("seq", "tp"),
        P("seq", None, None),
        P("seq", None, None),
        P(None, "tp", "seq", None),
        P(None, "tp", "seq", None),
    )
    return jax.shard_map(
        layer, mesh=mesh, in_specs=in_specs, out_specs=out_specs, check_vma=False
    )
```
